32 devices in a mesh: rep: 16 (over z, y, core), shard: 2 (over x).
Axes of the slice: x: 2, y: 2, z: 4, core: 2. Of those that a mesh axis runs over, the one named last changes fastest.
Arguments:
- token_in: bfloat16 [16384, 768], P(('rep', 'shard')), may hold values from -6 to 6
- char_in: bfloat16 [16384, 768], P(('rep', 'shard')), may hold values from -6 to 6
- char_ids: int32 [16384, 5], P(('rep', 'shard')), may hold values from 0 to 1023
- char_counts: int32 [16384], P(('rep', 'shard')), may hold values from 2 to 5
- segments: int32 [16384], P('rep'), may hold values from 0 to 63, never falling along the last dimension, each value on 1 to 512 neighbouring positions
- token_cot: bfloat16 [16384, 768], P(('rep', 'shard')), may hold values from -6 to 6
- char_cot: bfloat16 [16384, 768], P(('rep', 'shard')), may hold values from -6 to 6
- query_proj: float32 [768, 768], P('shard'), may hold values from -0.21875 to 0.21875
- key_proj: float32 [768, 768], P('shard'), may hold values from -0.21875 to 0.21875
- value_proj: float32 [768, 768], P('shard'), may hold values from -0.21875 to 0.21875
- output_proj: float32 [768, 768], P('shard'), may hold values from -1.75 to 1.75
- query_bias: float32 [768], P('shard'), may hold values from -1.2 to 1.2
- value_bias: float32 [768], P('shard'), may hold values from -1.2 to 1.2
- output_bias: float32 [768], P('shard'), may hold values from -1.2 to 1.2
- first_gain: float32 [768], P('shard'), may hold values from 0.5 to 1.5
- first_shift: float32 [768], P('shard'), may hold values from -1.2 to 1.2
- expand_proj: float32 [768, 3072], P('shard'), may hold values from -0.21875 to 0.21875
- expand_bias: float32 [3072], P('shard'), may hold values from -1.2 to 1.2
- shrink_proj: float32 [3072, 768], P('shard'), may hold values from -0.109375 to 0.109375
- shrink_bias: float32 [768], P('shard'), may hold values from -1.2 to 1.2
- char_table: float32 [1024, 256], P('shard'), may hold values from -6 to 6
- gate_input: float32 [2, 256, 1152], P(None, 'shard'), may hold values from -0.375 to 0.375
- input_bias: float32 [2, 1152], P(None, 'shard'), may hold values from -1.2 to 1.2
- gate_recur: float32 [2, 384, 1152], P(None, 'shard'), may hold values from -0.3125 to 0.3125
- recur_bias: float32 [2, 1152], P(None, 'shard'), may hold values from -1.2 to 1.2
- token_proj: float32 [768, 768], P('shard'), may hold values from -0.21875 to 0.21875
- token_bias: float32 [768], P('shard'), may hold values from -1.2 to 1.2
- char_proj: float32 [768, 768], P('shard'), may hold values from -0.21875 to 0.21875
- char_bias: float32 [768], P('shard'), may hold values from -1.2 to 1.2
- merging_kernel: float32 [3, 1536, 1536], P(None, 'shard'), may hold values from -0.09375 to 0.09375
- merging_bias: float32 [1536], P('shard'), may hold values from -1.2 to 1.2
- token_gain: float32 [768], P('shard'), may hold values from 0.5 to 1.5
- token_shift: float32 [768], P('shard'), may hold values from -1.2 to 1.2
- char_gain: float32 [768], P('shard'), may hold values from 0.5 to 1.5
- char_shift: float32 [768], P('shard'), may hold values from -1.2 to 1.2
Outputs:
- token_out: bfloat16 [16384, 768], P(('rep', 'shard'))
- char_out: bfloat16 [16384, 768], P(('rep', 'shard'))
- token_grad: float32 [16384, 768], P(('rep', 'shard'))
- char_grad: float32 [16384, 768], P(('rep', 'shard'))
- query_proj_grad: float32 [768, 768], P('shard')
- key_proj_grad: float32 [768, 768], P('shard')
- value_proj_grad: float32 [768, 768], P('shard')
- output_proj_grad: float32 [768, 768], P('shard')
- query_bias_grad: float32 [768], P('shard')
- value_bias_grad: float32 [768], P('shard')
- output_bias_grad: float32 [768], P('shard')
- first_gain_grad: float32 [768], P('shard')
- first_shift_grad: float32 [768], P('shard')
- expand_proj_grad: float32 [768, 3072], P('shard')
- expand_bias_grad: float32 [3072], P('shard')
- shrink_proj_grad: float32 [3072, 768], P('shard')
- shrink_bias_grad: float32 [768], P('shard')
- char_table_grad: float32 [1024, 256], P('shard')
- gate_input_grad: float32 [2, 256, 1152], P(None, 'shard')
- input_bias_grad: float32 [2, 1152], P(None, 'shard')
- gate_recur_grad: float32 [2, 384, 1152], P(None, 'shard')
- recur_bias_grad: float32 [2, 1152], P(None, 'shard')
- token_proj_grad: float32 [768, 768], P('shard')
- token_bias_grad: float32 [768], P('shard')
- char_proj_grad: float32 [768, 768], P('shard')
- char_bias_grad: float32 [768], P('shard')
- merging_kernel_grad: float32 [3, 1536, 1536], P(None, 'shard')
- merging_bias_grad: float32 [1536], P('shard')
- token_gain_grad: float32 [768], P('shard')
- token_shift_grad: float32 [768], P('shard')
- char_gain_grad: float32 [768], P('shard')
- char_shift_grad: float32 [768], P('shard')
The draws below stay inside these ranges and needn't reach their ends.
Inputs may be any that keep to these rules, and one draw needn't show every extreme that they name: `char_ids`: slots at or beyond a token's count in char_counts are never read. `segments`: segment numbers never fall along the tokens.
All inputs are finite; a program needn't handle non-finite values.
Results may differ from the reference program's by a relative error of at most 0.017.
The reference program's roundings to bfloat16 on the way (of `mixed` and `joined`) count: a program that leaves them out, or rounds other values in their place, can miss the bound.
Values may be sent and summed in bfloat16 or wider, within the bound.
No kernel may reach another device: no remote copies, remote signals or barrier semaphores. Data moves between devices by JAX's collectives and lax.ppermute only.
A program may use at most 640 MiB of HBM per device.

```python
import math
import jax
import jax.numpy as jnp
import numpy as np
from jax import lax

D = 768
HEADS = 12
HEAD_DIM = 64
FF = 3072
HID = 384
GATES = 1152
CHAR_DIM = 256
CHAR_VOCAB = 1024
SLOTS = 5
LENGTH = 1024
TOKENS = 16384


def set_ends(entries, own_key, low, largest):
    dims = entries.shape
    place = [jax.random.randint(jax.random.fold_in(own_key, axis), (), 0, dims[axis]) for axis in range(len(dims))]
    entries = entries.at[tuple(place)].set(low)
    longest = dims.index(max(dims))
    place[longest] = (place[longest] + 1) % dims[longest]
    return entries.at[tuple(place)].set(largest)


def level_of(own_key, extent, shards, least, high):
    loudness, own = 1.0, jax.random.fold_in(own_key, 6)
    for dim, shards_of in shards:
        heights = jnp.exp(jax.random.uniform(jax.random.fold_in(own, dim), (shards_of,), jnp.float32, least / len(shards), high / len(shards)))
        loudness = loudness * jnp.repeat(heights, extent[dim] // shards_of).reshape([-1 if axis == dim else 1 for axis in range(len(extent))])
    return loudness


def rank_table(number_of, slope):
    weights = [(1 << 20) // math.isqrt(grade ** slope) + 1 for grade in range(1, number_of + 1)]
    scale = 1 + sum(weights) // (1 << 30)
    return np.cumsum(np.array([max(1, weight // scale) for weight in weights]))


def ranked_ids(rng, extent, count, skew):
    grid = rank_table(count, skew)
    pick = jax.random.randint(jax.random.fold_in(rng, 1), extent, 0, int(grid[count - 1]))
    rank = jnp.searchsorted(jnp.asarray(grid, jnp.int32), pick, side="right")
    return jax.random.permutation(jax.random.fold_in(rng, 2), count)[rank].astype(jnp.int32)


def split_up(amount, total, reach, lean):
    portions = [(1 << 20) // math.isqrt(standing ** lean) + 1 for standing in range(2, amount + 1)]
    surplus, given = total - reach - (amount - 1), [1] * (amount - 1)
    while surplus > 0:
        candidates = [i for i in range(amount - 1) if given[i] < reach]
        pool, remaining = sum([portions[i] for i in candidates]), surplus
        for i in candidates:
            addition = min(reach - given[i], max(1, remaining * portions[i] // pool), surplus)
            given[i] = given[i] + addition
            surplus = surplus - addition
    return np.array([reach] + given)


def uneven(rng, number_of, total, bound, skew):
    if number_of == 2:
        one = jax.random.randint(rng, (), max(1, total - bound), min(bound, total - 1) + 1)
        return jnp.stack([one, total - one])
    sizes = jnp.asarray(split_up(number_of, total, bound, skew), jnp.int32)
    pairs = (number_of - 1) // 2
    donor, receiver = sizes[1:1 + 2 * pairs:2], sizes[2:2 + 2 * pairs:2]
    margin = jnp.minimum(donor - 1, bound - receiver)
    moved = jax.random.randint(jax.random.fold_in(rng, 1), (pairs,), 0, 1 << 20) % (margin + 1)
    sizes = sizes.at[1:1 + 2 * pairs:2].set(donor - moved).at[2:2 + 2 * pairs:2].set(receiver + moved)
    return sizes[jax.random.permutation(jax.random.fold_in(rng, 2), number_of)]


def normal_values(own_key, extent, deviation, limit, shards=(), kind=jnp.bfloat16):
    values = jax.random.normal(own_key, extent, jnp.float32) * deviation
    if len(shards) > 0:
        values = level_of(own_key, extent, shards, -0.22, 0.18) * values
    return jnp.clip(values, min=-limit, max=limit).astype(kind)


def setup_inputs(seed: int = 0) -> dict:
    seeds = jax.random.split(jax.random.key(seed), 36)
    return {
        "token_in": normal_values(seeds[0], (TOKENS, D), 1.0, 6.0, ((0, 32),)),
        "char_in": normal_values(seeds[1], (TOKENS, D), 1.0, 6.0, ((0, 32),)),
        "char_ids": set_ends(ranked_ids(seeds[2], (TOKENS, SLOTS), CHAR_VOCAB, 2), jax.random.fold_in(seeds[2], 3), 0, CHAR_VOCAB - 1).astype(jnp.int32),
        "char_counts": set_ends(jax.random.randint(seeds[3], (TOKENS,), 2, SLOTS + 1), jax.random.fold_in(seeds[3], 1), 2, SLOTS).astype(jnp.int32),
        "segments": jnp.searchsorted(jnp.cumsum(uneven(seeds[4], 4 * TOKENS // LENGTH, TOKENS, LENGTH // 2, 1)), jnp.arange(TOKENS), side="right").astype(jnp.int32),
        "token_cot": normal_values(seeds[5], (TOKENS, D), 1.0, 6.0, ((0, 32),)),
        "char_cot": normal_values(seeds[6], (TOKENS, D), 1.0, 6.0, ((0, 32),)),
        "query_proj": normal_values(seeds[7], (D, D), D ** -0.5, 0.21875, ((0, 2),), jnp.float32),
        "key_proj": normal_values(seeds[8], (D, D), D ** -0.5, 0.21875, ((0, 2),), jnp.float32),
        "value_proj": normal_values(seeds[9], (D, D), D ** -0.5, 0.21875, ((0, 2),), jnp.float32),
        "output_proj": normal_values(seeds[10], (D, D), (D // 64) ** -0.5, 1.75, ((0, 2),), jnp.float32),
        "query_bias": normal_values(seeds[11], (D,), 0.2, 1.2, ((0, 2),), jnp.float32),
        "value_bias": normal_values(seeds[12], (D,), 0.2, 1.2, ((0, 2),), jnp.float32),
        "output_bias": normal_values(seeds[13], (D,), 0.2, 1.2, ((0, 2),), jnp.float32),
        "first_gain": jnp.clip(1.0 + 0.1 * jax.random.normal(seeds[14], (D,), jnp.float32), 0.5, 1.5),
        "first_shift": normal_values(seeds[15], (D,), 0.2, 1.2, ((0, 2),), jnp.float32),
        "expand_proj": normal_values(seeds[16], (D, FF), D ** -0.5, 0.21875, ((0, 2),), jnp.float32),
        "expand_bias": normal_values(seeds[17], (FF,), 0.2, 1.2, ((0, 2),), jnp.float32),
        "shrink_proj": normal_values(seeds[18], (FF, D), FF ** -0.5, 0.109375, ((0, 2),), jnp.float32),
        "shrink_bias": normal_values(seeds[19], (D,), 0.2, 1.2, ((0, 2),), jnp.float32),
        "char_table": normal_values(seeds[20], (CHAR_VOCAB, CHAR_DIM), 1.0, 6.0, ((0, 2),), jnp.float32),
        "gate_input": normal_values(seeds[21], (2, CHAR_DIM, GATES), CHAR_DIM ** -0.5, 0.375, ((1, 2),), jnp.float32),
        "input_bias": normal_values(seeds[22], (2, GATES), 0.2, 1.2, ((1, 2),), jnp.float32),
        "gate_recur": normal_values(seeds[23], (2, HID, GATES), HID ** -0.5, 0.3125, ((1, 2),), jnp.float32),
        "recur_bias": normal_values(seeds[24], (2, GATES), 0.2, 1.2, ((1, 2),), jnp.float32),
        "token_proj": normal_values(seeds[25], (D, D), D ** -0.5, 0.21875, ((0, 2),), jnp.float32),
        "token_bias": normal_values(seeds[26], (D,), 0.2, 1.2, ((0, 2),), jnp.float32),
        "char_proj": normal_values(seeds[27], (2 * HID, D), (2 * HID) ** -0.5, 0.21875, ((0, 2),), jnp.float32),
        "char_bias": normal_values(seeds[28], (D,), 0.2, 1.2, ((0, 2),), jnp.float32),
        "merging_kernel": normal_values(seeds[29], (3, 2 * D, 2 * D), (6 * D) ** -0.5, 0.09375, ((1, 2),), jnp.float32),
        "merging_bias": normal_values(seeds[30], (2 * D,), 0.2, 1.2, ((0, 2),), jnp.float32),
        "token_gain": jnp.clip(1.0 + 0.1 * jax.random.normal(seeds[31], (D,), jnp.float32), 0.5, 1.5),
        "token_shift": normal_values(seeds[32], (D,), 0.2, 1.2, ((0, 2),), jnp.float32),
        "char_gain": jnp.clip(1.0 + 0.1 * jax.random.normal(seeds[33], (D,), jnp.float32), 0.5, 1.5),
        "char_shift": normal_values(seeds[34], (D,), 0.2, 1.2, ((0, 2),), jnp.float32),
    }


@jax.custom_vjp
def low(v):
    return lax.optimization_barrier(v.astype(jnp.bfloat16)).astype(jnp.float32)

@jax.custom_vjp
def low_back(v):
    return v

def low_keep(v):
    return (low(v), None)

def low_pass(kept, grad):
    return (grad,)

def back_keep(v):
    return (v, None)

def back_low(kept, grad):
    return (low(grad),)
low.defvjp(low_keep, low_pass)
low_back.defvjp(back_keep, back_low)
exact_mode = lax.Precision.HIGHEST
norm_eps = 1e-05
masked_score = -1000000000.0

def product(left, right):
    return jnp.dot(left, right, precision=exact_mode)

def layer_norm(values, gain, shift):
    centre = lax.optimization_barrier(jnp.mean(values, axis=-1, keepdims=True))
    centred = values - centre
    spread = lax.optimization_barrier(jnp.mean(centred * centred, axis=-1, keepdims=True))
    return centred * lax.rsqrt(spread + norm_eps) * gain + shift

def gelu_exact(values):
    return jax.nn.gelu(values, approximate=False)

def gates(step_in, recur):
    width = recur.shape[-1] // 3
    reset = jax.nn.sigmoid(step_in[..., :width] + recur[..., :width])
    update = jax.nn.sigmoid(step_in[..., width:2 * width] + recur[..., width:2 * width])
    candidate = jnp.tanh(step_in[..., 2 * width:] + reset * recur[..., 2 * width:])
    return (reset, update, candidate)

def letter_steps(ext_inputs, ext_counts, rows, slots):
    order = jnp.arange(slots)
    ahead = jnp.concatenate([ext_inputs[0, :rows], ext_inputs[0, 1:rows + 1]], axis=1)
    behind = jnp.concatenate([ext_inputs[1, 2:, ::-1], ext_inputs[1, 1:rows + 1, ::-1]], axis=1)
    step_in = jnp.stack([ahead, behind]).transpose(2, 0, 1, 3)
    ahead_mask = jnp.concatenate([order[None, :] < ext_counts[:rows, None], order[None, :] < ext_counts[1:rows + 1, None]], axis=1)
    reverse_order = order[::-1]
    behind_mask = jnp.concatenate([reverse_order[None, :] < ext_counts[2:, None], reverse_order[None, :] < ext_counts[1:rows + 1, None]], axis=1)
    step_mask = jnp.stack([ahead_mask, behind_mask]).astype(jnp.float32).transpose(2, 0, 1)
    return (step_in, step_mask)

def restarts(keep_ahead, keep_behind, slots):
    ones = jnp.ones((2 * slots, 2, keep_ahead.shape[0]), jnp.float32)
    return ones.at[slots].set(jnp.stack([keep_ahead, keep_behind]))

def attend_block(item, keys, values, seg_all):
    query_rows, seg_rows = item
    head_q = query_rows.reshape(-1, HEADS, HEAD_DIM)
    head_k = keys.reshape(-1, HEADS, HEAD_DIM)
    head_v = values.reshape(-1, HEADS, HEAD_DIM)
    scores = jnp.einsum('qhd,khd->hqk', head_q, head_k, precision=exact_mode) * HEAD_DIM ** (-0.5)
    scores = jnp.where(seg_rows[None, :, None] == seg_all[None, None, :], scores, masked_score)
    scores = low_back(scores)
    probs = low(jax.nn.softmax(scores, axis=-1))
    mixed = jnp.einsum('hqk,khd->qhd', probs, head_v, precision=exact_mode)
    return mixed.reshape(-1, D)

def forward_one(token_rows, char_rows, ids, counts, seg, params):
    query_proj, key_proj, value_proj, output_proj, query_bias, value_bias, output_bias, first_gain, first_shift, expand_proj, expand_bias, shrink_proj, shrink_bias, char_table, gate_input, input_bias, gate_recur, recur_bias, token_proj, token_bias, char_proj, char_bias, merging_kernel, merging_bias, token_gain, token_shift, char_gain, char_shift = [low(item) for item in params]
    queries = low_back(low(product(token_rows, query_proj) + query_bias))
    keys = low_back(low(product(token_rows, key_proj)))
    values = low_back(low(product(token_rows, value_proj) + value_bias))
    block = min(512, LENGTH)
    blocks = LENGTH // block

    def attend(item):
        return attend_block(item, keys, values, seg)
    mixed = lax.map(jax.checkpoint(attend), (queries.reshape(blocks, block, D), seg.reshape(blocks, block)))
    mixed = low_back(low(mixed.reshape(LENGTH, D)))
    attn = low_back(product(mixed, output_proj) + output_bias)
    first = layer_norm(token_rows + attn, first_gain, first_shift)
    up = low_back(product(low(first), expand_proj) + expand_bias)
    hidden = low(gelu_exact(up))
    token_mid = first + low_back(product(hidden, shrink_proj) + shrink_bias)
    embedded = char_table[ids]
    inputs = low_back(jnp.einsum('lsc,dcg->dlsg', embedded, gate_input, precision=exact_mode) + input_bias[:, None, None, :])
    inputs_ext = jnp.pad(inputs, ((0, 0), (1, 1), (0, 0), (0, 0)))
    counts_ext = jnp.pad(counts, (1, 1))
    step_in, step_mask = letter_steps(inputs_ext, counts_ext, LENGTH, SLOTS)
    position = jnp.arange(LENGTH)
    before = jnp.concatenate([seg[:1], seg[:-1]])
    after = jnp.concatenate([seg[1:], seg[-1:]])
    keep_ahead = ((position > 0) & (before == seg)).astype(jnp.float32)
    keep_behind = ((position < LENGTH - 1) & (after == seg)).astype(jnp.float32)
    restart = restarts(keep_ahead, keep_behind, SLOTS)

    def cell(state, item):
        one_in, one_mask, one_restart = item
        start = state * one_restart[..., None]
        recur = low_back(jnp.einsum('dlh,dhg->dlg', low(start), gate_recur, precision=exact_mode) + recur_bias[:, None, :])
        reset, update, candidate = gates(one_in, recur)
        fresh = (1.0 - update) * candidate + update * start
        mask = one_mask[..., None]
        return (mask * fresh + (1.0 - mask) * start, None)
    final_state, _ = lax.scan(cell, jnp.zeros((2, LENGTH, HID), jnp.float32), (step_in, step_mask, restart))
    pooled = jnp.concatenate([final_state[0], final_state[1]], axis=1)
    tok_side = low_back(product(low(token_mid), token_proj) + token_bias)
    char_side = low_back(product(low(pooled), char_proj) + char_bias)
    joined = low(jnp.concatenate([tok_side, char_side], axis=1))
    padded = jnp.pad(joined, ((1, 1), (0, 0)))
    merged = merging_bias + product(padded[0:LENGTH], merging_kernel[0]) + product(padded[1:LENGTH + 1], merging_kernel[1]) + product(padded[2:LENGTH + 2], merging_kernel[2])
    act = gelu_exact(low_back(merged))
    token_out = layer_norm(token_mid + act[:, :D], token_gain, token_shift)
    char_out = layer_norm(char_rows + act[:, D:], char_gain, char_shift)
    return (token_out, char_out)

def reference(token_in, char_in, char_ids, char_counts, segments, token_cot, char_cot, query_proj, key_proj, value_proj, output_proj, query_bias, value_bias, output_bias, first_gain, first_shift, expand_proj, expand_bias, shrink_proj, shrink_bias, char_table, gate_input, input_bias, gate_recur, recur_bias, token_proj, token_bias, char_proj, char_bias, merging_kernel, merging_bias, token_gain, token_shift, char_gain, char_shift):
    params = (query_proj, key_proj, value_proj, output_proj, query_bias, value_bias, output_bias, first_gain, first_shift, expand_proj, expand_bias, shrink_proj, shrink_bias, char_table, gate_input, input_bias, gate_recur, recur_bias, token_proj, token_bias, char_proj, char_bias, merging_kernel, merging_bias, token_gain, token_shift, char_gain, char_shift)
    sequences = TOKENS // LENGTH

    def shaped(values):
        return values.reshape((sequences, LENGTH) + values.shape[1:])

    def per_sequence(totals, item):
        token_rows, char_rows, ids, counts, seg, token_back, char_back = item

        def closed(token_rows, char_rows, params):
            return forward_one(token_rows, char_rows, ids, counts, seg, params)
        outputs, pullback = jax.vjp(closed, token_rows, char_rows, params)
        token_part, char_part, param_grads = pullback((token_back, char_back))
        totals = jax.tree.map(lambda left, right: left + right, totals, param_grads)
        return (totals, (outputs[0].astype(jnp.bfloat16), outputs[1].astype(jnp.bfloat16), token_part, char_part))
    zeros = tuple((jnp.zeros_like(item) for item in params))
    totals, (token_out, char_out, token_grad, char_grad) = lax.scan(per_sequence, zeros, (shaped(token_in.astype(jnp.float32)), shaped(char_in.astype(jnp.float32)), shaped(char_ids), shaped(char_counts), shaped(segments), shaped(token_cot.astype(jnp.float32)), shaped(char_cot.astype(jnp.float32))))
    return (token_out.reshape(TOKENS, D), char_out.reshape(TOKENS, D), token_grad.reshape(TOKENS, D), char_grad.reshape(TOKENS, D), totals[0], totals[1], totals[2], totals[3], totals[4], totals[5], totals[6], totals[7], totals[8], totals[9], totals[10], totals[11], totals[12], totals[13], totals[14], totals[15], totals[16], totals[17], totals[18], totals[19], totals[20], totals[21], totals[22], totals[23], totals[24], totals[25], totals[26], totals[27])
```

```python
import functools
import jax
import jax.numpy as jnp
from jax import lax
from jax.sharding import PartitionSpec as P
from jax.experimental import pallas as pl
from jax.experimental.pallas import tpu as pltpu

F32 = jnp.float32
BF16 = jnp.bfloat16
VMEM_BYTES = 60 * 1024 * 1024


def dot(left, right):
    return jnp.dot(left, right, preferred_element_type=F32)


def dot_nt(left, right):
    return lax.dot_general(left, right, (((1,), (1,)), ((), ())), preferred_element_type=F32)


def dot_tn(left, right):
    return lax.dot_general(left, right, (((0,), (0,)), ((), ())), preferred_element_type=F32)


def sigmoid(values):
    return 0.5 * jnp.tanh(0.5 * values) + 0.5


def chunks(rows):
    size = min(rows, 256)
    return [slice(start, start + size) for start in range(0, rows, size)]


def gru_specs(slots, rows, chars, gate_width, at):
    hid = gate_width // 3
    whole = lambda *shape: pl.BlockSpec(shape, lambda i: (0,) * len(shape))
    letters = lambda place: pl.BlockSpec((1, rows, chars), lambda i: (place(at(i)), 0, 0))
    last = slots - 1
    return [
        letters(lambda t: jnp.minimum(t, last)),
        letters(lambda t: jnp.maximum(last - t, 0)),
        letters(lambda t: jnp.maximum(t - slots, 0)),
        letters(lambda t: jnp.minimum(2 * slots - 1 - t, last)),
        whole(2, chars, gate_width),
        whole(2, hid, gate_width),
        whole(2, 1, gate_width),
        whole(2, 1, gate_width),
        whole(3, rows, 1),
        whole(2, rows, 1),
    ]


def gru_gates(letter, start_low, wi, wr, bi, br, hid):
    both = 2 * hid
    mixed = dot(letter, wi[:, :both]) + dot(start_low, wr[:, :both]) + (bi[:, :both] + br[:, :both])
    reset = sigmoid(mixed[:, :hid])
    update = sigmoid(mixed[:, hid:])
    carried = dot(start_low, wr[:, both:]) + br[:, both:]
    candidate = jnp.tanh(dot(letter, wi[:, both:]) + bi[:, both:] + reset * carried)
    return reset, update, candidate, carried


def gru_forward_kernel(slots, a0, a1, b0, b1, wi, wr, bi, br, counts, keep, starts, pooled, state):
    step = pl.program_id(0)
    rows, hid = state.shape[1], state.shape[2]

    @pl.when(step == 0)
    def _():
        state[...] = jnp.zeros_like(state)

    @pl.when(step == slots)
    def _():
        for way in range(2):
            state[way] = state[way] * keep[way]

    first = step < slots
    place = jnp.where(first, step, step - slots)
    for part in chunks(rows):
        for way, (near, own) in enumerate(((a0, b0), (a1, b1))):
            letter = jnp.where(first, near[0, part], own[0, part])
            start = state[way, part]
            starts[0, way, part] = start
            _, update, candidate, _ = gate_values = gru_gates(
                letter, start.astype(BF16), wi[way], wr[way], bi[way], br[way], hid
            )
            fresh = candidate + update * (start - candidate)
            slot = place if way == 0 else slots - 1 - place
            count = jnp.where(first, counts[way, part], counts[2, part])
            state[way, part] = jnp.where(slot < count, fresh, start)

    @pl.when(step == 2 * slots - 1)
    def _():
        for way in range(2):
            pooled[:, way * hid : (way + 1) * hid] = state[way].astype(BF16)


def gru_forward(letters, wi, wr, bi, br, counts, keep):
    near0, near1, own = letters
    slots, rows, chars = own.shape
    gate_width = wi.shape[-1]
    hid = gate_width // 3
    flops = 2 * 2 * slots * 2 * rows * (chars + hid) * gate_width
    return pl.pallas_call(
        functools.partial(gru_forward_kernel, slots),
        grid=(2 * slots,),
        in_specs=gru_specs(slots, rows, chars, gate_width, lambda i: i),
        out_specs=[
            pl.BlockSpec((1, 2, rows, hid), lambda i: (i, 0, 0, 0)),
            pl.BlockSpec((rows, 2 * hid), lambda i: (0, 0)),
        ],
        out_shape=[
            jax.ShapeDtypeStruct((2 * slots, 2, rows, hid), F32),
            jax.ShapeDtypeStruct((rows, 2 * hid), BF16),
        ],
        scratch_shapes=[pltpu.VMEM((2, rows, hid), F32)],
        compiler_params=pltpu.CompilerParams(vmem_limit_bytes=VMEM_BYTES),
        cost_estimate=pl.CostEstimate(
            flops=flops,
            bytes_accessed=2 * slots * 2 * rows * (hid * 4 + chars * 2),
            transcendentals=2 * slots * 2 * rows * gate_width,
        ),
        name="gru_forward",
    )(near0, near1, own, own, wi, wr, bi, br, counts, keep)


def gru_backward_kernel(
    slots, a0, a1, b0, b1, wi, wr, bi, br, counts, keep, starts, final, wi_t, wr_t,
    letter_grad, wi_grad, wr_grad, bi_grad, br_grad, state,
):
    back = pl.program_id(0)
    step = 2 * slots - 1 - back
    rows, hid = state.shape[1], state.shape[2]
    both = 2 * hid

    @pl.when(back == 0)
    def _():
        for way in range(2):
            state[way] = final[:, way * hid : (way + 1) * hid]
        wi_grad[...] = jnp.zeros_like(wi_grad)
        wr_grad[...] = jnp.zeros_like(wr_grad)
        bi_grad[...] = jnp.zeros_like(bi_grad)
        br_grad[...] = jnp.zeros_like(br_grad)

    first = step < slots
    place = jnp.where(first, step, step - slots)
    for part in chunks(rows):
        for way, (near, own) in enumerate(((a0, b0), (a1, b1))):
            letter = jnp.where(first, near[0, part], own[0, part])
            start = starts[0, way, part]
            start_low = start.astype(BF16)
            reset, update, candidate, carried = gru_gates(
                letter, start_low, wi[way], wr[way], bi[way], br[way], hid
            )
            slot = place if way == 0 else slots - 1 - place
            count = jnp.where(first, counts[way, part], counts[2, part])
            grad = state[way, part]
            fresh = jnp.where(slot < count, grad, 0.0)
            kept = grad - fresh
            scaled = fresh * (1.0 - update)
            cand_pre = scaled * (1.0 - candidate * candidate)
            update_pre = scaled * update * (start - candidate)
            cand_reset = cand_pre * reset
            reset_pre = cand_reset * carried * (1.0 - reset)
            shared = jnp.concatenate([reset_pre.astype(BF16), update_pre.astype(BF16)], axis=1)
            cand_in = cand_pre.astype(BF16)
            cand_rec = cand_reset.astype(BF16)
            state[way, part] = (
                kept
                + update * fresh
                + dot(shared, wr_t[way, :both])
                + dot(cand_rec, wr_t[way, both:])
            )
            letter_grad[0, way, part] = (
                dot(shared, wi_t[way, :both]) + dot(cand_in, wi_t[way, both:])
            ).astype(letter_grad.dtype)
            wi_grad[way, :, :both] += dot_tn(letter, shared)
            wi_grad[way, :, both:] += dot_tn(letter, cand_in)
            wr_grad[way, :, :both] += dot_tn(start_low, shared)
            wr_grad[way, :, both:] += dot_tn(start_low, cand_rec)
            total = jnp.sum(shared.astype(F32), axis=0, keepdims=True)
            bi_grad[way, :, :both] += total
            br_grad[way, :, :both] += total
            bi_grad[way, :, both:] += jnp.sum(cand_in.astype(F32), axis=0, keepdims=True)
            br_grad[way, :, both:] += jnp.sum(cand_rec.astype(F32), axis=0, keepdims=True)

    @pl.when(step == slots)
    def _():
        for way in range(2):
            state[way] = state[way] * keep[way]


def gru_backward(letters, wi, wr, bi, br, counts, keep, starts, final):
    near0, near1, own = letters
    slots, rows, chars = own.shape
    gate_width = wi.shape[-1]
    hid = gate_width // 3
    at = lambda i: 2 * slots - 1 - i
    flops = 3 * 2 * 2 * slots * 2 * rows * (chars + hid) * gate_width
    whole = lambda *shape: pl.BlockSpec(shape, lambda i: (0,) * len(shape))
    return pl.pallas_call(
        functools.partial(gru_backward_kernel, slots),
        grid=(2 * slots,),
        in_specs=gru_specs(slots, rows, chars, gate_width, at)
        + [
            pl.BlockSpec((1, 2, rows, hid), lambda i: (at(i), 0, 0, 0)),
            whole(rows, 2 * hid),
            whole(2, gate_width, chars),
            whole(2, gate_width, hid),
        ],
        out_specs=[
            pl.BlockSpec((1, 2, rows, chars), lambda i: (at(i), 0, 0, 0)),
            whole(2, chars, gate_width),
            whole(2, hid, gate_width),
            whole(2, 1, gate_width),
            whole(2, 1, gate_width),
        ],
        out_shape=[
            jax.ShapeDtypeStruct((2 * slots, 2, rows, chars), BF16),
            jax.ShapeDtypeStruct((2, chars, gate_width), F32),
            jax.ShapeDtypeStruct((2, hid, gate_width), F32),
            jax.ShapeDtypeStruct((2, 1, gate_width), F32),
            jax.ShapeDtypeStruct((2, 1, gate_width), F32),
        ],
        scratch_shapes=[pltpu.VMEM((2, rows, hid), F32)],
        compiler_params=pltpu.CompilerParams(vmem_limit_bytes=VMEM_BYTES),
        cost_estimate=pl.CostEstimate(
            flops=flops,
            bytes_accessed=2 * slots * 2 * rows * (hid * 4 + chars * 4),
            transcendentals=2 * slots * 2 * rows * gate_width,
        ),
        name="gru_backward",
    )(
        near0, near1, own, own, wi, wr, bi, br, counts, keep, starts, final,
        wi.transpose(0, 2, 1), wr.transpose(0, 2, 1),
    )


def head_masks(width, dtype, axis=1, other=1):
    lane = lax.broadcasted_iota(jnp.int32, (1, width) if axis == 1 else (width, 1), axis)
    low = (lane < width // 2).astype(dtype)
    return low, (1 - low).astype(dtype)


def attend_kernel(scale, q, k, v, seg_q, seg_k, out, logsum):
    pair = q.shape[1]
    half = pair // 2
    allowed = seg_k[...] == seg_q[...]
    lane = lax.broadcasted_iota(jnp.int32, (1, pair), 1)
    keys = k[...]
    values = v[...].T
    for head in range(2):
        mine = (lane < half) if head == 0 else (lane >= half)
        query = jnp.where(mine, q[...] * scale, 0).astype(BF16)
        scores = jnp.where(allowed, dot_nt(keys, query), -1e9)
        top = jnp.max(scores, axis=0, keepdims=True)
        expo = jnp.exp(scores - top)
        total = jnp.sum(expo, axis=0, keepdims=True)
        probs = (expo * (1.0 / total)).astype(BF16)
        logsum[0, head : head + 1, :] = top + jnp.log(total)
        mixed = dot(values[head * half : (head + 1) * half], probs)
        out[:, head * half : (head + 1) * half] = mixed.T.astype(BF16)


def attend(q, k, v, seg_q, seg_k, head_dim):
    rows, width = q.shape
    length = k.shape[0]
    pair = 2 * head_dim
    pairs = width // pair
    return pl.pallas_call(
        functools.partial(attend_kernel, head_dim ** -0.5),
        grid=(pairs,),
        in_specs=[
            pl.BlockSpec((rows, pair), lambda i: (0, i)),
            pl.BlockSpec((length, pair), lambda i: (0, i)),
            pl.BlockSpec((length, pair), lambda i: (0, i)),
            pl.BlockSpec((1, rows), lambda i: (0, 0)),
            pl.BlockSpec((length, 1), lambda i: (0, 0)),
        ],
        out_specs=[
            pl.BlockSpec((rows, pair), lambda i: (0, i)),
            pl.BlockSpec((1, 2, rows), lambda i: (i, 0, 0)),
        ],
        out_shape=[
            jax.ShapeDtypeStruct((rows, width), BF16),
            jax.ShapeDtypeStruct((pairs, 2, rows), F32),
        ],
        compiler_params=pltpu.CompilerParams(vmem_limit_bytes=VMEM_BYTES),
        cost_estimate=pl.CostEstimate(
            flops=16 * rows * length * width,
            bytes_accessed=4 * (rows + length) * width,
            transcendentals=rows * length * 2 * pairs,
        ),
        name="attend",
    )(q, k, v, seg_q, seg_k)


def attend_back_kernel(scale, q, k, v, seg_q, seg_k, grad, logsum, dq, dk, dv):
    pair = q.shape[1]
    half = pair // 2
    allowed = seg_k[...] == seg_q[...]
    lane = lax.broadcasted_iota(jnp.int32, (1, pair), 1)
    keys = k[...]
    values = v[...]
    keys_t = keys.T
    key_total = None
    value_total = None
    for head in range(2):
        mine = (lane < half) if head == 0 else (lane >= half)
        query = jnp.where(mine, q[...] * scale, 0).astype(BF16)
        out_grad = jnp.where(mine, grad[...], 0).astype(BF16)
        scores = jnp.where(allowed, dot_nt(keys, query), -1e9)
        probs = jnp.exp(scores - logsum[0, head : head + 1, :])
        probs_grad = dot_nt(values, out_grad)
        delta = jnp.sum(probs * probs_grad, axis=0, keepdims=True)
        scores_grad = (probs * (probs_grad - delta)).astype(BF16)
        key_part = dot(scores_grad, query)
        value_part = dot(probs.astype(BF16), out_grad)
        key_total = key_part if head == 0 else key_total + key_part
        value_total = value_part if head == 0 else value_total + value_part
        query_part = dot(keys_t[head * half : (head + 1) * half], scores_grad)
        dq[:, head * half : (head + 1) * half] = (query_part.T * scale).astype(BF16)
    dk[...] = key_total.astype(dk.dtype)
    dv[...] = value_total.astype(dv.dtype)


def attend_back(q, k, v, seg_q, seg_k, grad, logsum, head_dim):
    rows, width = q.shape
    length = k.shape[0]
    pair = 2 * head_dim
    pairs = width // pair
    return pl.pallas_call(
        functools.partial(attend_back_kernel, head_dim ** -0.5),
        grid=(pairs,),
        in_specs=[
            pl.BlockSpec((rows, pair), lambda i: (0, i)),
            pl.BlockSpec((length, pair), lambda i: (0, i)),
            pl.BlockSpec((length, pair), lambda i: (0, i)),
            pl.BlockSpec((1, rows), lambda i: (0, 0)),
            pl.BlockSpec((length, 1), lambda i: (0, 0)),
            pl.BlockSpec((rows, pair), lambda i: (0, i)),
            pl.BlockSpec((1, 2, rows), lambda i: (i, 0, 0)),
        ],
        out_specs=[
            pl.BlockSpec((rows, pair), lambda i: (0, i)),
            pl.BlockSpec((length, pair), lambda i: (0, i)),
            pl.BlockSpec((length, pair), lambda i: (0, i)),
        ],
        out_shape=[
            jax.ShapeDtypeStruct((rows, width), BF16),
            jax.ShapeDtypeStruct((length, width), BF16),
            jax.ShapeDtypeStruct((length, width), BF16),
        ],
        compiler_params=pltpu.CompilerParams(vmem_limit_bytes=VMEM_BYTES),
        cost_estimate=pl.CostEstimate(
            flops=40 * rows * length * width,
            bytes_accessed=6 * (rows + length) * width,
            transcendentals=rows * length * 2 * pairs,
        ),
        name="attend_back",
    )(q, k, v, seg_q, seg_k, grad, logsum)


HEAD_DIM = 64
PACK = 384
norm_eps = 1e-05


def layer_norm(values, gain, shift):
    centre = jnp.mean(values, axis=-1, keepdims=True)
    centred = values - centre
    spread = jnp.mean(centred * centred, axis=-1, keepdims=True)
    return centred * lax.rsqrt(spread + norm_eps) * gain + shift


def gelu_exact(values):
    return jax.nn.gelu(values, approximate=False)


def widen(values):
    return values.astype(F32)


def back_product(grad, weight):
    return jnp.einsum("rg,cg->rc", grad, weight, preferred_element_type=F32)


def flip(value, bit):
    count = lax.axis_size("rep")
    return lax.ppermute(value, "rep", [(i, i ^ bit) for i in range(count)])


def shift_shard(value, hop):
    count = lax.axis_size("shard")
    return lax.ppermute(value, "shard", [(i, (i - hop) % count) for i in range(count)])


def neighbour_rows(first, last):
    count, place = lax.axis_size("shard"), lax.axis_index("shard")
    if count == 2:
        got = lax.ppermute(jnp.where(place == 0, last, first), "shard", [(0, 1), (1, 0)])
        nothing = jnp.zeros_like(got)
        return jnp.where(place == 0, nothing, got), jnp.where(place == 0, got, nothing)
    up = [(i, i + 1) for i in range(count - 1)]
    down = [(i + 1, i) for i in range(count - 1)]
    return lax.ppermute(last, "shard", up), lax.ppermute(first, "shard", down)


def with_halo(value):
    before, after = neighbour_rows(value[:1], value[-1:])
    return jnp.concatenate([before, value, after], axis=0)


def gather_wide(master, dim):
    reps, rep = lax.axis_size("rep"), lax.axis_index("rep")
    rows = master.shape[dim]
    if rows % (8 * reps) == 0 or lax.axis_size("shard") != 2 and rows % reps == 0:
        piece = lax.dynamic_slice_in_dim(master, rep * (rows // reps), rows // reps, dim)
        return lax.all_gather(piece.astype(BF16), ("shard", "rep"), axis=dim, tiled=True)
    return lax.all_gather(master.astype(BF16), "shard", axis=dim, tiled=True)


def gather_small(value):
    if lax.axis_size("shard") != 2:
        return lax.all_gather(value, "shard")
    place = lax.axis_index("shard")
    other = lax.ppermute(value, "shard", [(0, 1), (1, 0)])
    return jnp.stack([jnp.where(place == 0, value, other), jnp.where(place == 0, other, value)])


def both_cores(*values):
    widths = [value.shape[1] for value in values]
    other = flip(jnp.concatenate(values, axis=1), 1)
    result, at = [], 0
    for value, width in zip(values, widths):
        result.append((value, other[:, at : at + width]))
        at += width
    return result


def core_half(value, which):
    half = value.shape[1] // 2
    return lax.dynamic_slice_in_dim(value, which * half, half, 1)


def pair_product(left, right):
    total = None
    for one, two in zip(left, right):
        part = jnp.einsum("rc,rg->cg", one, two, preferred_element_type=F32)
        total = part if total is None else total + part
    return total


def columns(pair, place, parts):
    size = pair[0].shape[1] // parts
    return [lax.dynamic_slice_in_dim(item, place * size, size, 1) for item in pair]


def packed(blocks, width):
    rows = []
    for block in blocks:
        lanes = block.shape[1]
        if lanes % width == 0:
            rows += [block[:, at : at + width] for at in range(0, lanes, width)]
        else:
            rows.append(block.reshape(-1, width))
    return jnp.concatenate(rows, axis=0) if len(rows) > 1 else rows[0]


def unpacked(rows, shapes, width):
    blocks, at = [], 0
    for depth, lanes in shapes:
        if lanes % width == 0:
            parts = []
            for _ in range(lanes // width):
                parts.append(rows[at : at + depth])
                at += depth
            blocks.append(jnp.concatenate(parts, axis=1) if len(parts) > 1 else parts[0])
        else:
            size = depth * lanes // width
            blocks.append(rows[at : at + size].reshape(depth, lanes))
            at += size
    return blocks


def reduce_group(build):
    parts, place = lax.axis_size("shard"), lax.axis_index("shard")
    rep = lax.axis_index("rep")
    sent = [
        shift_shard(build((place + hop) % parts).astype(BF16), hop * -1 % parts)
        for hop in range(1, parts)
    ]
    total = build(place)
    for item in sent:
        total = total + widen(item)
    bits = [1 << k for k in range(1, (lax.axis_size("rep") - 1).bit_length())]
    for bit in bits:
        half = total.shape[0] // 2
        side = (rep // bit) % 2
        away = lax.dynamic_slice_in_dim(total, (1 - side) * half, half, 0).astype(BF16)
        mine = lax.dynamic_slice_in_dim(total, side * half, half, 0)
        total = widen(mine) + widen(flip(away, bit))
    total = total.astype(BF16)
    for bit in bits[::-1]:
        other = flip(total, bit)
        side = (rep // bit) % 2
        total = jnp.concatenate(
            [jnp.where(side == 0, total, other), jnp.where(side == 0, other, total)], axis=0
        )
    other = flip(total, 1)
    core = rep % 2
    return jnp.where(core == 0, total, other), jnp.where(core == 0, other, total)


def shards(
    token_in,
    char_in,
    char_ids,
    char_counts,
    segments,
    token_cot,
    char_cot,
    query_proj,
    key_proj,
    value_proj,
    output_proj,
    query_bias,
    value_bias,
    output_bias,
    first_gain,
    first_shift,
    expand_proj,
    expand_bias,
    shrink_proj,
    shrink_bias,
    char_table,
    gate_input,
    input_bias,
    gate_recur,
    recur_bias,
    token_proj,
    token_bias,
    char_proj,
    char_bias,
    merging_kernel,
    merging_bias,
    token_gain,
    token_shift,
    char_gain,
    char_shift,
):
    rows, width = token_in.shape
    place, parts = lax.axis_index("shard"), lax.axis_size("shard")
    rep = lax.axis_index("rep")
    core = rep % 2
    slots = char_ids.shape[1]
    chars = char_table.shape[1]
    vocab = char_table.shape[0] * parts
    gate_width = gate_input.shape[-1]
    hid = gate_width // 3
    ff = expand_proj.shape[1]

    vectors = (
        query_bias, value_bias, output_bias, first_gain, first_shift, expand_bias, shrink_bias,
        input_bias, recur_bias, token_bias, char_bias, merging_bias, token_gain, token_shift,
        char_gain, char_shift,
    )
    flat = jnp.concatenate([item.reshape(-1) for item in vectors]).astype(BF16)
    pad = -flat.shape[0] % (8 * chars)
    small = jnp.concatenate(
        [char_table.astype(BF16), jnp.pad(flat, (0, pad)).reshape(-1, chars)], axis=0
    )
    small = gather_small(small)
    table_low = small[:, : char_table.shape[0]].reshape(vocab, chars)
    tail = widen(small[:, char_table.shape[0] :].reshape(parts, -1))
    wide, at = [], 0
    for item in vectors:
        size = item.size
        block = tail[:, at : at + size].reshape((parts,) + item.shape)
        at += size
        if item.ndim == 2:
            wide.append(block.transpose(1, 0, 2).reshape(item.shape[0], 1, -1))
        else:
            wide.append(block.reshape(-1))
    (
        bias_query, bias_value, bias_output, gain_first, shift_first, bias_expand, bias_shrink,
        bias_input, bias_recur, bias_token, bias_char, bias_merging, gain_token, shift_token,
        gain_char, shift_char,
    ) = wide

    qkv_low = gather_wide(jnp.stack([query_proj, key_proj, value_proj]), 1)
    query_low, key_low, value_low = qkv_low[0], qkv_low[1], qkv_low[2]
    input_low = gather_wide(gate_input, 1)
    recur_low = gather_wide(gate_recur, 1)
    side_low = gather_wide(jnp.stack([output_proj, token_proj, char_proj]), 1)
    output_low, project_token, project_char = side_low[0], side_low[1], side_low[2]
    expand_low = gather_wide(expand_proj, 0)
    shrink_low = gather_wide(shrink_proj, 0)
    kernel_low = gather_wide(merging_kernel, 1)

    queries = (dot(token_in, query_low) + bias_query).astype(BF16)
    keys = dot(token_in, key_low).astype(BF16)
    values = (dot(token_in, value_low) + bias_value).astype(BF16)
    keys_values = jnp.concatenate([keys, values], axis=1)
    blocks = [keys_values] + [shift_shard(keys_values, hop) for hop in range(1, parts)]
    everyone = jnp.concatenate(blocks, axis=0)
    seg_blocks = [
        lax.dynamic_slice_in_dim(segments, ((place + hop) % parts) * rows, rows)
        for hop in range(parts)
    ]
    seg_rows = seg_blocks[0]
    seg_q = seg_rows[None, :]
    seg_k = jnp.concatenate(seg_blocks)[:, None]
    all_keys, all_values = everyone[:, :width], everyone[:, width:]
    mixed, logsum = attend(queries, all_keys, all_values, seg_q, seg_k, HEAD_DIM)

    packed_ids = jnp.concatenate([char_ids, char_counts[:, None]], axis=1)
    ids_ext = with_halo(packed_ids)
    counts_ext = ids_ext[:, slots]
    onehot = (
        ids_ext[:, :slots].T.reshape(-1)[:, None] == jnp.arange(vocab, dtype=jnp.int32)[None, :]
    ).astype(BF16)
    embedded = dot(onehot, table_low).astype(BF16).reshape(slots, rows + 2, chars)
    letters = (embedded[:, :rows], embedded[:, 2:], embedded[:, 1 : rows + 1])
    counts = jnp.stack([counts_ext[:rows], counts_ext[2:], counts_ext[1 : rows + 1]])[:, :, None]
    length = segments.shape[0]
    position = place * rows + jnp.arange(rows)
    before = jnp.take(segments, jnp.maximum(position - 1, 0))
    after = jnp.take(segments, jnp.minimum(position + 1, length - 1))
    keep = jnp.stack(
        [
            ((position > 0) & (before == seg_rows)).astype(F32),
            ((position < length - 1) & (after == seg_rows)).astype(F32),
        ]
    )[:, :, None]
    starts, pooled_low = gru_forward(
        letters, input_low, recur_low, bias_input, bias_recur, counts, keep
    )

    first_in = widen(token_in) + (dot(mixed, output_low) + bias_output)
    first = layer_norm(first_in, gain_first, shift_first)
    first_low = first.astype(BF16)
    up = dot(first_low, expand_low) + bias_expand
    hidden = gelu_exact(up).astype(BF16)
    token_mid = first + dot(hidden, shrink_low) + bias_shrink
    mid_low = token_mid.astype(BF16)

    tok_side = dot(mid_low, project_token) + bias_token
    char_side = dot(pooled_low, project_char) + bias_char
    joined = jnp.concatenate([tok_side, char_side], axis=1).astype(BF16)
    joined_ext = with_halo(joined)
    merged = (
        bias_merging
        + dot(joined_ext[0:rows], kernel_low[0])
        + dot(joined_ext[1 : rows + 1], kernel_low[1])
        + dot(joined_ext[2 : rows + 2], kernel_low[2])
    )
    act = gelu_exact(merged)
    tok_pre = token_mid + act[:, :width]
    char_pre = widen(char_in) + act[:, width:]
    token_out = layer_norm(tok_pre, gain_token, shift_token).astype(BF16)
    char_out = layer_norm(char_pre, gain_char, shift_char).astype(BF16)

    _, token_pull = jax.vjp(layer_norm, tok_pre, gain_token, shift_token)
    tok_pre_grad, token_gain_grad, token_shift_grad = token_pull(widen(token_cot))
    _, char_pull = jax.vjp(layer_norm, char_pre, gain_char, shift_char)
    char_grad, char_gain_grad, char_shift_grad = char_pull(widen(char_cot))
    _, gelu_pull = jax.vjp(gelu_exact, merged)
    merged_grad = gelu_pull(jnp.concatenate([tok_pre_grad, char_grad], axis=1))[0].astype(BF16)
    merging_bias_grad = jnp.sum(widen(merged_grad), axis=0)
    joined_pair, merged_pair = both_cores(
        joined_ext, jnp.pad(core_half(merged_grad, 1 - core), ((0, 2), (0, 0)))
    )
    merged_pair = (core_half(merged_grad, core), merged_pair[1][:rows])

    def merging_terms(target):
        sources = columns(joined_pair, target, parts)
        return jnp.concatenate(
            [
                pair_product([item[tap : tap + rows] for item in sources], merged_pair)
                for tap in range(3)
            ],
            axis=0,
        )

    merging_sum = reduce_group(merging_terms)
    merged_ext = with_halo(merged_grad)
    joined_grad = (
        back_product(merged_ext[2 : rows + 2], kernel_low[0])
        + back_product(merged_ext[1 : rows + 1], kernel_low[1])
        + back_product(merged_ext[0:rows], kernel_low[2])
    )
    tok_side_grad = joined_grad[:, :width].astype(BF16)
    char_side_grad = joined_grad[:, width:].astype(BF16)
    token_bias_grad = jnp.sum(widen(tok_side_grad), axis=0)
    char_bias_grad = jnp.sum(widen(char_side_grad), axis=0)
    pooled_grad = back_product(char_side_grad, project_char)
    mid_grad = tok_pre_grad + back_product(tok_side_grad, project_token)

    shrink_out_grad = mid_grad.astype(BF16)
    shrink_bias_grad = jnp.sum(widen(shrink_out_grad), axis=0)
    hidden_grad = back_product(shrink_out_grad, shrink_low)
    _, up_pull = jax.vjp(gelu_exact, up)
    up_grad = up_pull(hidden_grad)[0].astype(BF16)
    expand_bias_grad = jnp.sum(widen(up_grad), axis=0)
    first_grad = mid_grad + back_product(up_grad, expand_low)
    halves = (shrink_out_grad, up_grad, tok_side_grad, char_side_grad)
    pairs = both_cores(
        hidden, first_low, mid_low, pooled_low, *[core_half(item, 1 - core) for item in halves]
    )
    mine = [(core_half(item, core), pair[1]) for item, pair in zip(halves, pairs[4:])]

    def middle_terms(target):
        return packed(
            [
                pair_product(columns(pairs[0], target, parts), mine[0]),
                pair_product(mine[1], columns(pairs[1], target, parts)),
                pair_product(columns(pairs[2], target, parts), mine[2]),
                pair_product(columns(pairs[3], target, parts), mine[3]),
            ],
            PACK,
        )

    middle_sum = reduce_group(middle_terms)

    _, first_pull = jax.vjp(layer_norm, first_in, gain_first, shift_first)
    first_in_grad, first_gain_grad, first_shift_grad = first_pull(first_grad)
    attn_grad = first_in_grad.astype(BF16)
    output_bias_grad = jnp.sum(widen(attn_grad), axis=0)
    mixed_grad = back_product(attn_grad, output_low).astype(BF16)
    queries_grad, key_terms, value_terms = attend_back(
        queries, all_keys, all_values, seg_q, seg_k, mixed_grad, logsum, HEAD_DIM
    )
    terms = jnp.concatenate([key_terms, value_terms], axis=1)
    owned = widen(terms[:rows])
    for hop in range(1, parts):
        owned = owned + widen(shift_shard(terms[hop * rows : (hop + 1) * rows], -hop % parts))
    owned = owned.astype(BF16)

    letter_grad, input_grad, recur_grad, bias_input_grad, bias_recur_grad = gru_backward(
        letters, input_low, recur_low, bias_input, bias_recur, counts, keep, starts, pooled_grad
    )
    ahead, behind = widen(letter_grad[:, 0]), widen(letter_grad[:, 1])
    embedded_grad = (
        jnp.pad(ahead[:slots], ((0, 0), (0, 2), (0, 0)))
        + jnp.pad(behind[:slots][::-1], ((0, 0), (2, 0), (0, 0)))
        + jnp.pad(ahead[slots:] + behind[slots:][::-1], ((0, 0), (1, 1), (0, 0)))
    )
    table_grad = dot_tn(onehot, embedded_grad.astype(BF16).reshape(-1, chars))

    keys_grad, values_grad = owned[:, :width], owned[:, width:]
    query_bias_grad = jnp.sum(widen(queries_grad), axis=0)
    value_bias_grad = jnp.sum(widen(values_grad), axis=0)
    token_grad = (
        first_in_grad
        + back_product(queries_grad, query_low)
        + back_product(keys_grad, key_low)
        + back_product(values_grad, value_low)
    )

    late = (queries_grad, keys_grad, values_grad, attn_grad)
    late_pairs = both_cores(token_in, mixed, *[core_half(item, 1 - core) for item in late])
    late_mine = [(core_half(item, core), pair[1]) for item, pair in zip(late, late_pairs[2:])]
    gru_terms = jnp.concatenate([input_grad, recur_grad], axis=1)
    gru_away = lax.dynamic_index_in_dim(gru_terms, 1 - core, 0, keepdims=False).astype(BF16)
    gru_own = lax.dynamic_index_in_dim(gru_terms, core, 0, keepdims=False) + widen(flip(gru_away, 1))
    table_terms = table_grad.reshape(parts, 2, -1, chars)
    table_away = lax.dynamic_index_in_dim(table_terms, 1 - core, 1, keepdims=False).astype(BF16)
    table_own = lax.dynamic_index_in_dim(table_terms, core, 1, keepdims=False) + widen(
        flip(table_away, 1)
    )
    chars_part, hid_part = chars // parts, hid // parts

    def late_terms(target):
        table_part = lax.dynamic_index_in_dim(table_own, target, 0, keepdims=False)
        return packed(
            [
                pair_product(columns(late_pairs[0], target, parts), late_mine[0]),
                pair_product(columns(late_pairs[0], target, parts), late_mine[1]),
                pair_product(columns(late_pairs[0], target, parts), late_mine[2]),
                pair_product(columns(late_pairs[1], target, parts), late_mine[3]),
                lax.dynamic_slice_in_dim(gru_own, target * chars_part, chars_part, 0),
                lax.dynamic_slice_in_dim(gru_own, chars + target * hid_part, hid_part, 0),
                jnp.pad(table_part, ((0, 0), (0, PACK - chars))),
            ],
            PACK,
        )

    late_sum = reduce_group(late_terms)

    vector_grads = (
        query_bias_grad, value_bias_grad, output_bias_grad, first_gain_grad, first_shift_grad,
        expand_bias_grad, shrink_bias_grad, bias_input_grad[:, 0], bias_recur_grad[:, 0],
        token_bias_grad, char_bias_grad, merging_bias_grad, token_gain_grad, token_shift_grad,
        char_gain_grad, char_shift_grad,
    )
    flat_grad = jnp.concatenate([item.reshape(-1) for item in vector_grads])
    flat_grad = jnp.pad(flat_grad, (0, -flat_grad.shape[0] % 1024)).reshape(-1, 128)
    flat_grad = lax.psum(flat_grad, ("rep", "shard")).reshape(-1)
    vector_out, at = [], 0
    for item in vector_grads:
        full = flat_grad[at : at + item.size].reshape(item.shape)
        at += item.size
        size = item.shape[-1] // parts
        vector_out.append(lax.dynamic_slice_in_dim(full, place * size, size, item.ndim - 1))
    (
        query_bias_out, value_bias_out, output_bias_out, first_gain_out, first_shift_out,
        expand_bias_out, shrink_bias_out, input_bias_out, recur_bias_out, token_bias_out,
        char_bias_out, merging_bias_out, token_gain_out, token_shift_out, char_gain_out,
        char_shift_out,
    ) = vector_out

    part, joint = width // parts, 2 * width // parts
    merging_out = jnp.concatenate(
        [widen(half).reshape(3, joint, width) for half in merging_sum], axis=2
    )
    middle = [
        unpacked(half, [(ff // parts, PACK), (ff // 2, part), (part, PACK), (part, PACK)], PACK)
        for half in middle_sum
    ]
    shrink_out = jnp.concatenate([widen(half[0]) for half in middle], axis=1)
    expand_out = jnp.concatenate([widen(half[1]) for half in middle], axis=0).T
    token_proj_out = jnp.concatenate([widen(half[2]) for half in middle], axis=1)
    char_proj_out = jnp.concatenate([widen(half[3]) for half in middle], axis=1)
    tail_rows = vocab // parts // 2
    late_blocks = [
        unpacked(
            half,
            [(part, PACK)] * 4
            + [(chars_part, gate_width), (hid_part, gate_width), (tail_rows, PACK)],
            PACK,
        )
        for half in late_sum
    ]
    query_out, key_out, value_out, output_out = [
        jnp.concatenate([widen(half[k]) for half in late_blocks], axis=1) for k in range(4)
    ]
    input_out = jnp.stack([widen(half[4]) for half in late_blocks])
    recur_out = jnp.stack([widen(half[5]) for half in late_blocks])
    table_out = jnp.concatenate([widen(half[6][:, :chars]) for half in late_blocks], axis=0)
    return (
        token_out, char_out, token_grad, char_grad,
        query_out, key_out, value_out, output_out,
        query_bias_out, value_bias_out, output_bias_out, first_gain_out, first_shift_out,
        expand_out, expand_bias_out, shrink_out, shrink_bias_out, table_out,
        input_out, input_bias_out, recur_out, recur_bias_out,
        token_proj_out, token_bias_out, char_proj_out, char_bias_out,
        merging_out, merging_bias_out, token_gain_out, token_shift_out, char_gain_out,
        char_shift_out,
    )


def solution(mesh):
    rows = P(("rep", "shard"), None)
    split, vector = P("shard", None), P("shard")
    in_specs = (
        rows, rows, rows, P(("rep", "shard")), P("rep"), rows, rows,
        split, split, split, split, vector, vector, vector, vector, vector,
        split, vector, split, vector, split,
        P(None, "shard", None), P(None, "shard"), P(None, "shard", None), P(None, "shard"),
        split, vector, split, vector, P(None, "shard", None), vector,
        vector, vector, vector, vector,
    )
    out_specs = (rows,) * 4 + in_specs[7:]
    return jax.shard_map(shards, mesh=mesh, in_specs=in_specs, out_specs=out_specs, check_vma=False)
```

```python
import functools
import jax
import jax.numpy as jnp
from jax import lax
from jax.sharding import PartitionSpec as P
from jax.experimental import pallas as pl
from jax.experimental.pallas import tpu as pltpu

F32 = jnp.float32
BF16 = jnp.bfloat16
VMEM_BYTES = 60 * 1024 * 1024
LIGHT = pl.CostEstimate(flops=1024, bytes_accessed=1024, transcendentals=0)


def dot(left, right):
    return jnp.dot(left, right, preferred_element_type=F32)


def dot_nt(left, right):
    return lax.dot_general(left, right, (((1,), (1,)), ((), ())), preferred_element_type=F32)


def dot_tn(left, right):
    return lax.dot_general(left, right, (((0,), (0,)), ((), ())), preferred_element_type=F32)


def sigmoid(values):
    return 0.5 * jnp.tanh(0.5 * values) + 0.5


def chunks(rows):
    size = min(rows, 256)
    return [slice(start, start + size) for start in range(0, rows, size)]


def gru_specs(slots, rows, chars, gate_width, at):
    hid = gate_width // 3
    whole = lambda *shape: pl.BlockSpec(shape, lambda i: (0,) * len(shape))
    letters = lambda place: pl.BlockSpec((1, rows, chars), lambda i: (place(at(i)), 0, 0))
    last = slots - 1
    return [
        letters(lambda t: jnp.minimum(t, last)),
        letters(lambda t: jnp.maximum(last - t, 0)),
        letters(lambda t: jnp.maximum(t - slots, 0)),
        letters(lambda t: jnp.minimum(2 * slots - 1 - t, last)),
        whole(2, chars, gate_width),
        whole(2, hid, gate_width),
        whole(2, 1, gate_width),
        whole(2, 1, gate_width),
        whole(3, rows, 1),
        whole(2, rows, 1),
    ]


def gru_gates(letter, start_low, wi, wr, bi, br, hid):
    both = 2 * hid
    mixed = dot(letter, wi[:, :both]) + dot(start_low, wr[:, :both]) + (bi[:, :both] + br[:, :both])
    reset = sigmoid(mixed[:, :hid])
    update = sigmoid(mixed[:, hid:])
    carried = dot(start_low, wr[:, both:]) + br[:, both:]
    candidate = jnp.tanh(dot(letter, wi[:, both:]) + bi[:, both:] + reset * carried)
    return reset, update, candidate, carried


def gru_forward_kernel(slots, a0, a1, b0, b1, wi, wr, bi, br, counts, keep, starts, pooled, state):
    step = pl.program_id(0)
    rows, hid = state.shape[1], state.shape[2]

    @pl.when(step == 0)
    def _():
        state[...] = jnp.zeros_like(state)

    @pl.when(step == slots)
    def _():
        for way in range(2):
            state[way] = state[way] * keep[way]

    first = step < slots
    place = jnp.where(first, step, step - slots)
    for part in chunks(rows):
        for way, (near, own) in enumerate(((a0, b0), (a1, b1))):
            letter = jnp.where(first, near[0, part], own[0, part])
            start = state[way, part]
            starts[0, way, part] = start
            _, update, candidate, _ = gate_values = gru_gates(
                letter, start.astype(BF16), wi[way], wr[way], bi[way], br[way], hid
            )
            fresh = candidate + update * (start - candidate)
            slot = place if way == 0 else slots - 1 - place
            count = jnp.where(first, counts[way, part], counts[2, part])
            state[way, part] = jnp.where(slot < count, fresh, start)

    @pl.when(step == 2 * slots - 1)
    def _():
        for way in range(2):
            pooled[:, way * hid : (way + 1) * hid] = state[way].astype(BF16)


def gru_forward(letters, wi, wr, bi, br, counts, keep):
    near0, near1, own = letters
    slots, rows, chars = own.shape
    gate_width = wi.shape[-1]
    hid = gate_width // 3
    return pl.pallas_call(
        functools.partial(gru_forward_kernel, slots),
        grid=(2 * slots,),
        in_specs=gru_specs(slots, rows, chars, gate_width, lambda i: i),
        out_specs=[
            pl.BlockSpec((1, 2, rows, hid), lambda i: (i, 0, 0, 0)),
            pl.BlockSpec((rows, 2 * hid), lambda i: (0, 0)),
        ],
        out_shape=[
            jax.ShapeDtypeStruct((2 * slots, 2, rows, hid), F32),
            jax.ShapeDtypeStruct((rows, 2 * hid), BF16),
        ],
        scratch_shapes=[pltpu.VMEM((2, rows, hid), F32)],
        compiler_params=pltpu.CompilerParams(vmem_limit_bytes=VMEM_BYTES),
        cost_estimate=LIGHT,
        name="gru_forward",
    )(near0, near1, own, own, wi, wr, bi, br, counts, keep)


def gru_backward_kernel(slots, last, x0, x1, wi, wr, bi, br, counts, keep, starts, final, *refs):
    sums, refs = (None, refs) if last else (refs[:4], refs[4:])
    letter_grads, (start_grad, wi_grad, wr_grad, bi_grad, br_grad) = refs[:2], refs[2:]
    back = pl.program_id(0)
    place = slots - 1 - back
    rows, hid = final.shape[1], final.shape[2]
    both = 2 * hid

    @pl.when(back == 0)
    def _():
        start_grad[...] = final[...]
        for k, total in enumerate((wi_grad, wr_grad, bi_grad, br_grad)):
            total[...] = jnp.zeros_like(total) if last else sums[k][...]

    for part in chunks(rows):
        for way, letters in enumerate((x0, x1)):
            letter = letters[0, part]
            start = starts[0, way, part]
            start_low = start.astype(BF16)
            reset, update, candidate, carried = gru_gates(
                letter, start_low, wi[way], wr[way], bi[way], br[way], hid
            )
            slot = place if way == 0 else slots - 1 - place
            grad = start_grad[way, part]
            fresh = jnp.where(slot < counts[way, part], grad, 0.0)
            kept = grad - fresh
            scaled = fresh * (1.0 - update)
            cand_pre = scaled * (1.0 - candidate * candidate)
            update_pre = scaled * update * (start - candidate)
            cand_reset = cand_pre * reset
            reset_pre = cand_reset * carried * (1.0 - reset)
            shared = jnp.concatenate([reset_pre.astype(BF16), update_pre.astype(BF16)], axis=1)
            cand_in = cand_pre.astype(BF16)
            cand_rec = cand_reset.astype(BF16)
            start_grad[way, part] = (
                kept
                + update * fresh
                + dot_nt(shared, wr[way, :, :both])
                + dot_nt(cand_rec, wr[way, :, both:])
            )
            letter_grads[way][0, part] = (
                dot_nt(shared, wi[way, :, :both]) + dot_nt(cand_in, wi[way, :, both:])
            ).astype(BF16)
            wi_grad[way, :, :both] += dot_tn(letter, shared)
            wi_grad[way, :, both:] += dot_tn(letter, cand_in)
            wr_grad[way, :, :both] += dot_tn(start_low, shared)
            wr_grad[way, :, both:] += dot_tn(start_low, cand_rec)
            total = jnp.sum(shared.astype(F32), axis=0, keepdims=True)
            bi_grad[way, :, :both] += total
            br_grad[way, :, :both] += total
            bi_grad[way, :, both:] += jnp.sum(cand_in.astype(F32), axis=0, keepdims=True)
            br_grad[way, :, both:] += jnp.sum(cand_rec.astype(F32), axis=0, keepdims=True)

    if last:

        @pl.when(back == slots - 1)
        def _():
            for way in range(2):
                start_grad[way] = start_grad[way] * keep[way]


def gru_backward(last, near0, near1, wi, wr, bi, br, counts, keep, starts, final, sums=()):
    slots, rows, chars = near0.shape
    gate_width = wi.shape[-1]
    hid = gate_width // 3
    offset = slots if last else 0
    whole = lambda *shape: pl.BlockSpec(shape, lambda i: (0,) * len(shape))
    return pl.pallas_call(
        functools.partial(gru_backward_kernel, slots, last),
        grid=(slots,),
        in_specs=[
            pl.BlockSpec((1, rows, chars), lambda i: (slots - 1 - i, 0, 0)),
            pl.BlockSpec((1, rows, chars), lambda i: (i, 0, 0)),
            whole(2, chars, gate_width),
            whole(2, hid, gate_width),
            whole(2, 1, gate_width),
            whole(2, 1, gate_width),
            whole(2, rows, 1),
            whole(2, rows, 1),
            pl.BlockSpec((1, 2, rows, hid), lambda i: (offset + slots - 1 - i, 0, 0, 0)),
            whole(2, rows, hid),
        ]
        + [whole(*item.shape) for item in sums],
        out_specs=[
            pl.BlockSpec((1, rows, chars), lambda i: (slots - 1 - i, 0, 0)),
            pl.BlockSpec((1, rows, chars), lambda i: (i, 0, 0)),
            whole(2, rows, hid),
            whole(2, chars, gate_width),
            whole(2, hid, gate_width),
            whole(2, 1, gate_width),
            whole(2, 1, gate_width),
        ],
        out_shape=[
            jax.ShapeDtypeStruct((slots, rows, chars), BF16),
            jax.ShapeDtypeStruct((slots, rows, chars), BF16),
            jax.ShapeDtypeStruct((2, rows, hid), F32),
            jax.ShapeDtypeStruct((2, chars, gate_width), F32),
            jax.ShapeDtypeStruct((2, hid, gate_width), F32),
            jax.ShapeDtypeStruct((2, 1, gate_width), F32),
            jax.ShapeDtypeStruct((2, 1, gate_width), F32),
        ],
        compiler_params=pltpu.CompilerParams(vmem_limit_bytes=VMEM_BYTES),
        cost_estimate=LIGHT,
        name="gru_backward",
    )(near0, near1, wi, wr, bi, br, counts, keep, starts, final, *sums)


def half_spec(item, place):
    if item.ndim == 3:
        return pl.BlockSpec((1,) + item.shape[1:], lambda i, w: (place(i, w)[0], place(i, w)[1], 0))
    rows, lanes = item.shape
    return pl.BlockSpec((rows, lanes // 2), lambda i, w: (place(i, w)[1], place(i, w)[0]))


def flat2(ref):
    return ref.at[0] if len(ref.shape) == 3 else ref


def pack_kernel(width, where, *refs):
    out, at = refs[-1], 0
    for ref in refs[:-1]:
        item = flat2(ref)
        rows, lanes = item.shape
        for lane in range(0, lanes, width):
            out[at : at + rows, :] = item[:, lane : lane + width].astype(BF16)
            at += rows


def pack_halves(core, masters, width):
    total = sum(item.size for item in masters) // 2 // width
    where = jnp.stack([core, core])
    return pl.pallas_call(
        functools.partial(pack_kernel, width),
        grid_spec=pltpu.PrefetchScalarGridSpec(
            num_scalar_prefetch=1,
            grid=(1,),
            in_specs=[half_spec(item, lambda i, w: (w[0], 0)) for item in masters],
            out_specs=pl.BlockSpec((total, width), lambda i, w: (0, 0)),
        ),
        out_shape=jax.ShapeDtypeStruct((total, width), BF16),
        compiler_params=pltpu.CompilerParams(vmem_limit_bytes=VMEM_BYTES),
        cost_estimate=LIGHT,
        name="pack_halves",
    )(where, *masters)


def table_kernel(ids, near0, near1, own0, own1, out):
    @pl.when(pl.program_id(0) == 0)
    def _():
        out[...] = jnp.zeros_like(out)

    own = (own0[0].astype(F32) + own1[0].astype(F32)).astype(BF16)
    rows, vocab = own.shape[0], out.shape[0]
    letters = lax.broadcasted_iota(jnp.int32, (rows, vocab), 1)
    total = None
    for which, grad in enumerate((near0[0], near1[0], own)):
        chosen = jnp.where(ids[which, 0] == letters, 1.0, 0.0).astype(BF16)
        part = dot_tn(chosen, grad)
        total = part if total is None else total + part
    out[...] += total


def table_terms_of(ids, near0, near1, own0, own1, vocab):
    slots, rows, chars = near0.shape
    one = pl.BlockSpec((1, rows, chars), lambda i: (i, 0, 0))
    return pl.pallas_call(
        table_kernel,
        grid=(slots,),
        in_specs=[pl.BlockSpec((3, 1, rows, 1), lambda i: (0, i, 0, 0)), one, one, one, one],
        out_specs=pl.BlockSpec((vocab, chars), lambda i: (0, 0)),
        out_shape=jax.ShapeDtypeStruct((vocab, chars), F32),
        compiler_params=pltpu.CompilerParams(vmem_limit_bytes=VMEM_BYTES),
        cost_estimate=LIGHT,
        name="table_terms",
    )(ids, near0, near1, own0, own1)


def block_terms_kernel(table, a0, b0, a1, b1, out):
    out[...] = (dot_tn(a0[...], b0[...]) + dot_tn(a1[...], b1[...])).astype(out.dtype)


def block_terms(left, right, table, width, dtype):
    rows, count = left[0].shape[0], table.shape[1]
    one = pl.BlockSpec((rows, width), lambda i, t: (0, t[0, i]))
    if right[0].ndim == 3:
        across = right[0].shape[2] // width
        two = pl.BlockSpec(
            (None, rows, width), lambda i, t: (t[1, i] // across, 0, t[1, i] % across)
        )
    else:
        two = pl.BlockSpec((rows, width), lambda i, t: (0, t[1, i]))
    return pl.pallas_call(
        block_terms_kernel,
        grid_spec=pltpu.PrefetchScalarGridSpec(
            num_scalar_prefetch=1,
            grid=(count,),
            in_specs=[one, two, one, two],
            out_specs=pl.BlockSpec((width, width), lambda i, t: (i, 0)),
        ),
        out_shape=jax.ShapeDtypeStruct((count * width, width), dtype),
        compiler_params=pltpu.CompilerParams(vmem_limit_bytes=VMEM_BYTES),
        cost_estimate=LIGHT,
        name="block_terms",
    )(table, left[0], right[0], left[1], right[1])


def unpack_kernel(shapes, where, mine, other, *outs):
    width = mine.shape[1]
    for turn, source in ((0, mine), (1, other)):

        @pl.when(pl.program_id(0) == turn)
        def _(source=source):
            at = 0
            for (rows, lanes, kind), out in zip(shapes, outs):
                if kind == "turned":
                    out[...] = source[at : at + rows, :].astype(F32).T
                    at += rows
                    continue
                target = out.at[0] if kind == "stacked" else out
                for lane in range(0, lanes, width):
                    some = min(width, lanes - lane)
                    target[:, lane : lane + some] = source[at : at + rows, :some].astype(F32)
                    at += rows


def unpack_halves(core, mine, other, shapes):
    where = jnp.stack([core, core])
    half = lambda i, w: jnp.where(i == 0, w[0], 1 - w[0])
    specs, outs = [], []
    for rows, lanes, kind in shapes:
        if kind == "lanes":
            specs.append(pl.BlockSpec((rows, lanes), lambda i, w: (0, half(i, w))))
            outs.append((rows, 2 * lanes))
        elif kind == "stacked":
            specs.append(pl.BlockSpec((1, rows, lanes), lambda i, w: (half(i, w), 0, 0)))
            outs.append((2, rows, lanes))
        elif kind == "rows":
            specs.append(pl.BlockSpec((rows, lanes), lambda i, w: (half(i, w), 0)))
            outs.append((2 * rows, lanes))
        else:
            specs.append(pl.BlockSpec((lanes, rows), lambda i, w: (0, half(i, w))))
            outs.append((lanes, 2 * rows))
    whole = pl.BlockSpec(mine.shape, lambda i, w: (0, 0))
    return pl.pallas_call(
        functools.partial(unpack_kernel, shapes),
        grid_spec=pltpu.PrefetchScalarGridSpec(
            num_scalar_prefetch=1, grid=(2,), in_specs=[whole, whole], out_specs=specs
        ),
        out_shape=[jax.ShapeDtypeStruct(item, F32) for item in outs],
        compiler_params=pltpu.CompilerParams(vmem_limit_bytes=VMEM_BYTES),
        cost_estimate=LIGHT,
        name="unpack_halves",
    )(where, mine, other)


def rows_kernel(width, *refs):
    out, at = refs[-1], 0
    for ref in refs[:-1]:
        rows, lanes = ref.shape
        for lane in range(0, lanes, width):
            out[at : at + rows, :] = ref[:, lane : lane + width].astype(out.dtype)
            at += rows


def pack_rows(blocks, width, dtype):
    blocks = [item if item.shape[1] % width == 0 else item.reshape(-1, width) for item in blocks]
    total = sum(item.size for item in blocks) // width
    return pl.pallas_call(
        functools.partial(rows_kernel, width),
        out_shape=jax.ShapeDtypeStruct((total, width), dtype),
        compiler_params=pltpu.CompilerParams(vmem_limit_bytes=VMEM_BYTES),
        cost_estimate=LIGHT,
        name="pack_rows",
    )(*blocks)


def gru_terms_kernel(width, where, *refs):
    out = refs[-1]
    sums, table, vectors = refs[:-3], refs[-3], refs[-2]
    parts = out.shape[0]
    out[...] = jnp.zeros_like(out)
    for part in range(parts):
        at = 0
        for item in sums:
            rows = item.shape[1] // parts
            rest = slice(part * rows, (part + 1) * rows)
            for lane in range(0, item.shape[2], width):
                out[part, at : at + rows, :] = item[0, rest, lane : lane + width].astype(out.dtype)
                at += rows
        rows, lanes = table.shape[2], table.shape[3]
        out[part, at : at + rows, :lanes] = table[part, 0].astype(out.dtype)
        at += rows
        rows = vectors.shape[2]
        out[part, at : at + rows, :] = vectors[part, 0].astype(out.dtype)


def pack_gru_terms(which, sums, table, vectors, depth, width, dtype):
    parts = table.shape[0]
    where = jnp.stack([which, which])
    chosen = lambda item: pl.BlockSpec((1,) + item.shape[1:], lambda i, w: (w[0], 0, 0))
    second = lambda item: pl.BlockSpec(
        (parts, 1) + item.shape[2:], lambda i, w: (0, w[0], 0, 0)
    )
    return pl.pallas_call(
        functools.partial(gru_terms_kernel, width),
        grid_spec=pltpu.PrefetchScalarGridSpec(
            num_scalar_prefetch=1,
            grid=(1,),
            in_specs=[chosen(item) for item in sums] + [second(table), second(vectors)],
            out_specs=pl.BlockSpec((parts, depth, width), lambda i, w: (0, 0, 0)),
        ),
        out_shape=jax.ShapeDtypeStruct((parts, depth, width), dtype),
        compiler_params=pltpu.CompilerParams(vmem_limit_bytes=VMEM_BYTES),
        cost_estimate=LIGHT,
        name="pack_gru_terms",
    )(where, *sums, table, vectors)


def join_kernel(width, count, where, *refs):
    step = pl.program_id(0)
    masters, (mine, peer), outs = refs[:count], refs[count : count + 2], refs[count + 2 :]

    @pl.when(step < 2)
    def _():
        for master, out in zip(masters, outs):
            out[...] = master[...].astype(BF16)

    for turn, source in ((2, mine), (3, peer)):

        @pl.when(step == turn)
        def _(source=source):
            at = 0
            for out in outs:
                item = flat2(out)
                rows, lanes = item.shape
                for lane in range(0, lanes, width):
                    item[:, lane : lane + width] = source[at : at + rows, :]
                    at += rows


def join_halves(place, core, masters, mine, peer, width):
    where = jnp.stack([place, core])

    def source(i, w):
        return (jnp.minimum(i, 1), 0)

    def target(i, w):
        half = jnp.where(i < 2, i, jnp.where(i == 2, w[1], 1 - w[1]))
        return (half, jnp.where(i < 2, w[0], 1 - w[0]))

    def wide(item):
        return item.shape[:-2] + (2 * item.shape[-2], item.shape[-1])

    rows = pl.BlockSpec(mine.shape, lambda i, w: (0, 0))
    return pl.pallas_call(
        functools.partial(join_kernel, width, len(masters)),
        grid_spec=pltpu.PrefetchScalarGridSpec(
            num_scalar_prefetch=1,
            grid=(4,),
            in_specs=[half_spec(item, source) for item in masters] + [rows, rows],
            out_specs=[half_spec(item, target) for item in masters],
        ),
        out_shape=[jax.ShapeDtypeStruct(wide(item), BF16) for item in masters],
        compiler_params=pltpu.CompilerParams(vmem_limit_bytes=VMEM_BYTES),
        cost_estimate=LIGHT,
        name="join_halves",
    )(where, *masters, mine, peer)


def attend_kernel(scale, q, k, v, seg_q, seg_k, out, logsum):
    pair = q.shape[1]
    half = pair // 2
    allowed = seg_k[...] == seg_q[...]
    lane = lax.broadcasted_iota(jnp.int32, (1, pair), 1)
    keys = k[...]
    values = v[...].T
    for head in range(2):
        mine = (lane < half) if head == 0 else (lane >= half)
        query = jnp.where(mine, q[...] * scale, 0).astype(BF16)
        scores = jnp.where(allowed, dot_nt(keys, query), -1e9)
        top = jnp.max(scores, axis=0, keepdims=True)
        expo = jnp.exp(scores - top)
        total = jnp.sum(expo, axis=0, keepdims=True)
        probs = (expo * (1.0 / total)).astype(BF16)
        logsum[0, head : head + 1, :] = top + jnp.log(total)
        mixed = dot(values[head * half : (head + 1) * half], probs)
        out[:, head * half : (head + 1) * half] = mixed.T.astype(BF16)


def attend(q, k, v, seg_q, seg_k, head_dim):
    rows, width = q.shape
    length = k.shape[0]
    pair = 2 * head_dim
    pairs = width // pair
    return pl.pallas_call(
        functools.partial(attend_kernel, head_dim ** -0.5),
        grid=(pairs,),
        in_specs=[
            pl.BlockSpec((rows, pair), lambda i: (0, i)),
            pl.BlockSpec((length, pair), lambda i: (0, i)),
            pl.BlockSpec((length, pair), lambda i: (0, i)),
            pl.BlockSpec((1, rows), lambda i: (0, 0)),
            pl.BlockSpec((length, 1), lambda i: (0, 0)),
        ],
        out_specs=[
            pl.BlockSpec((rows, pair), lambda i: (0, i)),
            pl.BlockSpec((1, 2, rows), lambda i: (i, 0, 0)),
        ],
        out_shape=[
            jax.ShapeDtypeStruct((rows, width), BF16),
            jax.ShapeDtypeStruct((pairs, 2, rows), F32),
        ],
        compiler_params=pltpu.CompilerParams(vmem_limit_bytes=VMEM_BYTES),
        cost_estimate=LIGHT,
        name="attend",
    )(q, k, v, seg_q, seg_k)


def attend_back_kernel(scale, q, k, v, seg_q, seg_k, grad, logsum, dq, *terms):
    pair = q.shape[1]
    half = pair // 2
    allowed = seg_k[...] == seg_q[...]
    lane = lax.broadcasted_iota(jnp.int32, (1, pair), 1)
    keys = k[...]
    values = v[...]
    keys_t = keys.T
    key_total = None
    value_total = None
    for head in range(2):
        mine = (lane < half) if head == 0 else (lane >= half)
        query = jnp.where(mine, q[...] * scale, 0).astype(BF16)
        out_grad = jnp.where(mine, grad[...], 0).astype(BF16)
        scores = jnp.where(allowed, dot_nt(keys, query), -1e9)
        probs = jnp.exp(scores - logsum[0, head : head + 1, :])
        probs_grad = dot_nt(values, out_grad)
        delta = jnp.sum(probs * probs_grad, axis=0, keepdims=True)
        scores_grad = (probs * (probs_grad - delta)).astype(BF16)
        key_part = dot(scores_grad, query)
        value_part = dot(probs.astype(BF16), out_grad)
        key_total = key_part if head == 0 else key_total + key_part
        value_total = value_part if head == 0 else value_total + value_part
        query_part = dot(keys_t[head * half : (head + 1) * half], scores_grad)
        dq[:, head * half : (head + 1) * half] = (query_part.T * scale).astype(BF16)
    for part, out in enumerate(terms):
        rows = slice(part * out.shape[1], (part + 1) * out.shape[1])
        out[0] = key_total[rows].astype(BF16)
        out[1] = value_total[rows].astype(BF16)


def attend_back(q, k, v, seg_q, seg_k, grad, logsum, head_dim):
    rows, width = q.shape
    length = k.shape[0]
    pair = 2 * head_dim
    pairs = width // pair
    return pl.pallas_call(
        functools.partial(attend_back_kernel, head_dim ** -0.5),
        grid=(pairs,),
        in_specs=[
            pl.BlockSpec((rows, pair), lambda i: (0, i)),
            pl.BlockSpec((length, pair), lambda i: (0, i)),
            pl.BlockSpec((length, pair), lambda i: (0, i)),
            pl.BlockSpec((1, rows), lambda i: (0, 0)),
            pl.BlockSpec((length, 1), lambda i: (0, 0)),
            pl.BlockSpec((rows, pair), lambda i: (0, i)),
            pl.BlockSpec((1, 2, rows), lambda i: (i, 0, 0)),
        ],
        out_specs=[
            pl.BlockSpec((rows, pair), lambda i: (0, i)),
        ]
        + [pl.BlockSpec((2, rows, pair), lambda i: (0, 0, i))] * (length // rows),
        out_shape=[jax.ShapeDtypeStruct((rows, width), BF16)]
        + [jax.ShapeDtypeStruct((2, rows, width), BF16)] * (length // rows),
        compiler_params=pltpu.CompilerParams(vmem_limit_bytes=VMEM_BYTES),
        cost_estimate=LIGHT,
        name="attend_back",
    )(q, k, v, seg_q, seg_k, grad, logsum)


HEAD_DIM = 64
PACK = 384
TAIL = "adbcdacdbcdabcdbdb"
norm_eps = 1e-05


def layer_norm(values, gain, shift):
    centre = jnp.mean(values, axis=-1, keepdims=True)
    centred = values - centre
    spread = jnp.mean(centred * centred, axis=-1, keepdims=True)
    return centred * lax.rsqrt(spread + norm_eps) * gain + shift


ERFC = (
    -1.26551223, 1.00002368, 0.37409196, 0.09678418, -0.18628806, 0.27886807, -1.13520398,
    1.48851587, -0.82215223, 0.17087277,
)


def normal_share(values):
    size = jnp.abs(values) * (0.5 ** 0.5)
    place = 1.0 / (1.0 + 0.5 * size)
    power = ERFC[-1]
    for term in ERFC[-2::-1]:
        power = power * place + term
    tail = 0.5 * place * jnp.exp(power - size * size)
    return jnp.where(values < 0, tail, 1.0 - tail)


def gelu_exact(values):
    return values * normal_share(values)


def gelu_slope(values):
    return normal_share(values) + values * jnp.exp(-0.5 * values * values) * 0.3989422804014327


def widen(values):
    return values.astype(F32)


def back_product(grad, weight):
    return jnp.einsum("rg,cg->rc", grad, weight, preferred_element_type=F32)


def rep_size():
    return 2 * lax.axis_size("pair")


def rep_index():
    return 2 * lax.axis_index("pair") + lax.axis_index("core")


def flip(value, bit):
    if bit == 1:
        return lax.ppermute(value, "core", [(0, 1), (1, 0)])
    count = lax.axis_size("pair")
    return lax.ppermute(value, "pair", [(i, i ^ (bit // 2)) for i in range(count)])


def shift_shard(value, hop):
    count = lax.axis_size("shard")
    return lax.ppermute(value, "shard", [(i, (i - hop) % count) for i in range(count)])


def neighbour_rows(first, last):
    count, place = lax.axis_size("shard"), lax.axis_index("shard")
    if count == 2:
        got = lax.ppermute(jnp.where(place == 0, last, first), "shard", [(0, 1), (1, 0)])
        nothing = jnp.zeros_like(got)
        return jnp.where(place == 0, nothing, got), jnp.where(place == 0, got, nothing)
    up = [(i, i + 1) for i in range(count - 1)]
    down = [(i + 1, i) for i in range(count - 1)]
    return lax.ppermute(last, "shard", up), lax.ppermute(first, "shard", down)


def with_halo(value):
    before, after = neighbour_rows(value[:1], value[-1:])
    return jnp.concatenate([before, value, after], axis=0)


def small_pieces(masters):
    fits = all(item.shape[-2] % (8 * rep_size()) == 0 for item in masters)
    return fits and lax.axis_size("shard") == 2


def own_piece(master):
    rows = master.shape[-2] // rep_size()
    return lax.dynamic_slice_in_dim(master, rep_index() * rows, rows, master.ndim - 2).astype(BF16)


def in_order(piece, other):
    first = lax.axis_index("shard") == 0
    return jnp.stack([jnp.where(first, piece, other), jnp.where(first, other, piece)])


def gather_shard(master):
    return lax.all_gather(master.astype(BF16), "shard", axis=master.ndim - 2, tiled=True)


class Fetch:
    def __init__(self, masters, spread=False):
        self.masters = masters
        self.alone = lax.axis_size("shard") != 2
        self.spread = spread and rep_size() > 2
        self.core = rep_index() % 2
        self.side = rep_index() // 2 % 2
        if self.alone:
            self.state = [gather_shard(item) for item in masters]
            return
        self.state = pack_halves(self.core, masters, PACK)
        if self.spread:
            half = self.state.shape[0] // 2
            self.state = lax.dynamic_slice_in_dim(self.state, self.side * half, half, 0)

    def cross(self):
        if not self.alone:
            self.state = shift_shard(self.state, 1)

    def share(self):
        if not self.alone and self.spread:
            self.state = (self.state, flip(self.state, 2))

    def swap(self):
        if self.alone:
            return
        if self.spread:
            mine, other = self.state
            self.state = jnp.concatenate(
                [
                    jnp.where(self.side == 0, mine, other),
                    jnp.where(self.side == 0, other, mine),
                ],
                axis=0,
            )
        self.state = (self.state, flip(self.state, 1))

    def whole(self):
        if self.alone:
            return self.state
        place = lax.axis_index("shard")
        return join_halves(place, self.core, self.masters, *self.state, PACK)


def land(fetches, *values):
    states, values = lax.optimization_barrier(([item.state for item in fetches], values))
    for item, state in zip(fetches, states):
        item.state = state
    return values


def gather_small(value):
    if lax.axis_size("shard") != 2:
        return lax.all_gather(value, "shard")
    place = lax.axis_index("shard")
    other = lax.ppermute(value, "shard", [(0, 1), (1, 0)])
    return jnp.stack([jnp.where(place == 0, value, other), jnp.where(place == 0, other, value)])


def both_cores(*values):
    widths = [value.shape[1] for value in values]
    other = flip(jnp.concatenate(values, axis=1), 1)
    result, at = [], 0
    for value, width in zip(values, widths):
        result.append((value, other[:, at : at + width]))
        at += width
    return result


def core_half(value, which):
    half = value.shape[1] // 2
    return lax.dynamic_slice_in_dim(value, which * half, half, 1)


def pair_product(left, right):
    total = None
    for one, two in zip(left, right):
        part = jnp.einsum("rc,rg->cg", one, two, preferred_element_type=F32)
        total = part if total is None else total + part
    return total


def columns(pair, place, parts):
    size = pair[0].shape[1] // parts
    return [lax.dynamic_slice_in_dim(item, place * size, size, 1) for item in pair]


def weights_of(pair, shapes):
    core, width = lax.axis_index("core"), pair[0].shape[1]
    if all(lanes % width == 0 or kind == "rows" for _, lanes, kind in shapes):
        return unpack_halves(core, *pair, shapes)
    low, high = [jnp.where(core == k, pair[0], pair[1]) for k in range(2)]
    blocks, at = [], 0
    for rows, lanes, kind in shapes:
        if kind == "rows":
            halves = [half[at : at + rows, :lanes] for half in (low, high)]
            at += rows
        elif lanes % width:
            size = rows * lanes // width
            halves = [half[at : at + size].reshape(rows, lanes) for half in (low, high)]
            at += size
        else:
            count = lanes // width
            halves = [
                jnp.concatenate(
                    [half[at + k * rows : at + (k + 1) * rows] for k in range(count)], axis=1
                )
                for half in (low, high)
            ]
            at += count * rows
        halves = [widen(half) for half in halves]
        if kind == "stacked":
            blocks.append(jnp.stack(halves))
        elif kind == "turned":
            blocks.append(jnp.concatenate(halves, axis=0).T)
        else:
            blocks.append(jnp.concatenate(halves, axis=1 if kind == "lanes" else 0))
    return blocks


class Flow:
    def __init__(self, sent, value):
        self.value, self.away = value, sent
        bits = [1 << k for k in range(1, (rep_size() - 1).bit_length())]
        self.stages = [("shard", 0)] + [("halve", bit) for bit in bits]
        self.stages += [("double", bit) for bit in bits[::-1]] + [("core", 1)]
        if len(bits) > 1:
            self.stages[2:-2] = [("scatter", 0), ("gather", 0)]

    def launch(self):
        kind, bit = self.stages[0]
        if kind == "shard":
            parts = lax.axis_size("shard")
            self.got = [shift_shard(item, -hop % parts) for hop, item in enumerate(self.away, 1)]
        elif kind in ("scatter", "gather"):
            self.got = [flip(item, 4 * hop) for hop, item in enumerate(self.away, 1)]
        else:
            self.got = [flip(item, bit) for item in self.away]

    @staticmethod
    def by_place(items):
        whole, z = jnp.stack(items), rep_index() // 4
        return [
            lax.dynamic_index_in_dim(whole, jnp.bitwise_xor(z, p), 0, keepdims=False)
            for p in range(len(items))
        ]

    def combine(self):
        kind, bit = self.stages.pop(0)
        side = (rep_index() // max(bit, 1)) % 2
        if kind in ("shard", "halve", "scatter"):
            total = widen(self.value)
            for item in self.got:
                total = total + widen(item)
            self.value = total.astype(BF16)
        elif kind == "core":
            self.value = (self.value, self.got[0])
        elif kind == "gather":
            self.value = jnp.concatenate(self.by_place([self.value] + self.got), axis=0)
        else:
            low = jnp.where(side == 0, self.value, self.got[0])
            high = jnp.where(side == 0, self.got[0], self.value)
            self.value = jnp.concatenate([low, high], axis=0)
        if not self.stages:
            return
        kind, bit = self.stages[0]
        if kind in ("scatter", "gather"):
            count = rep_size() // 4
            self.away = [self.value] * (count - 1)
            if kind == "scatter":
                rows = self.value.shape[0] // count
                self.value, *self.away = self.by_place(
                    [self.value[k * rows : (k + 1) * rows] for k in range(count)]
                )
        elif kind == "halve":
            half = self.value.shape[0] // 2
            side = (rep_index() // bit) % 2
            self.away = [lax.dynamic_slice_in_dim(self.value, (1 - side) * half, half, 0)]
            self.value = lax.dynamic_slice_in_dim(self.value, side * half, half, 0)
        else:
            self.away = [self.value]


def turn(token, landing, starting, *values):
    landing = [flow for flow in landing if flow.stages]
    got, values, token = lax.optimization_barrier(([flow.got for flow in landing], values, token))
    for flow, item in zip(landing, got):
        flow.got = item
        flow.combine()
    going = [flow for flow in landing if flow.stages] + list(starting)
    away, values, token = lax.optimization_barrier(([flow.away for flow in going], values, token))
    for flow, item in zip(going, away):
        flow.away = item
        flow.launch()
    return token, values


def shards(
    token_in,
    char_in,
    char_ids,
    char_counts,
    segments,
    token_cot,
    char_cot,
    query_proj,
    key_proj,
    value_proj,
    output_proj,
    query_bias,
    value_bias,
    output_bias,
    first_gain,
    first_shift,
    expand_proj,
    expand_bias,
    shrink_proj,
    shrink_bias,
    char_table,
    gate_input,
    input_bias,
    gate_recur,
    recur_bias,
    token_proj,
    token_bias,
    char_proj,
    char_bias,
    merging_kernel,
    merging_bias,
    token_gain,
    token_shift,
    char_gain,
    char_shift,
):
    rows, width = token_in.shape
    place, parts = lax.axis_index("shard"), lax.axis_size("shard")
    rep = rep_index()
    core = rep % 2
    slots = char_ids.shape[1]
    chars = char_table.shape[1]
    vocab = char_table.shape[0] * parts
    gate_width = gate_input.shape[-1]
    hid = gate_width // 3
    ff = expand_proj.shape[1]

    first_fetch = Fetch([query_proj, key_proj, value_proj])
    gate_input, gate_recur, merging_kernel, flat_first = land(
        [first_fetch], gate_input, gate_recur, merging_kernel, query_bias
    )
    first_fetch.cross()
    spread = small_pieces([merging_kernel])
    kernel_piece = own_piece(merging_kernel) if spread else jnp.zeros((8, 128), BF16)
    gate_fetch = Fetch([gate_input, gate_recur])

    vectors = (
        flat_first, value_bias, output_bias, first_gain, first_shift, expand_bias, shrink_bias,
        input_bias, recur_bias, token_bias, char_bias, merging_bias, token_gain, token_shift,
        char_gain, char_shift,
    )
    flat = jnp.concatenate([item.reshape(-1) for item in vectors]).astype(BF16)
    pad = -flat.shape[0] % (8 * chars)
    small = jnp.concatenate(
        [char_table.astype(BF16), jnp.pad(flat, (0, pad)).reshape(-1, chars)], axis=0
    )
    packed_ids = jnp.concatenate([char_ids, char_counts[:, None]], axis=1)
    small, packed_ids, kernel_piece = land([first_fetch, gate_fetch], small, packed_ids, kernel_piece)
    gate_fetch.cross()
    first_fetch.swap()
    kernel_other = shift_shard(kernel_piece, 1) if spread else kernel_piece
    small = gather_small(small)
    ids_ext = with_halo(packed_ids)
    query_low, key_low, value_low = first_fetch.whole()
    table_low = small[:, : char_table.shape[0]].reshape(vocab, chars)
    tail = widen(small[:, char_table.shape[0] :].reshape(parts, -1))
    wide, at = [], 0
    for item in vectors:
        size = item.size
        block = tail[:, at : at + size].reshape((parts,) + item.shape)
        at += size
        if item.ndim == 2:
            wide.append(block.transpose(1, 0, 2).reshape(item.shape[0], 1, -1))
        else:
            wide.append(block.reshape(-1))
    (
        bias_query, bias_value, bias_output, gain_first, shift_first, bias_expand, bias_shrink,
        bias_input, bias_recur, bias_token, bias_char, bias_merging, gain_token, shift_token,
        gain_char, shift_char,
    ) = wide

    counts_ext = ids_ext[:, slots]
    onehot = (
        ids_ext[:, :slots].T.reshape(-1)[:, None] == jnp.arange(vocab, dtype=jnp.int32)[None, :]
    ).astype(BF16)
    letters_of = [ids_ext[at : at + rows, :slots].T for at in (0, 2, 1)]
    id_columns = jnp.stack(letters_of)[..., None]
    counts = jnp.stack([counts_ext[:rows], counts_ext[2:], counts_ext[1 : rows + 1]])[:, :, None]
    length = segments.shape[0]
    seg_blocks = [
        lax.dynamic_slice_in_dim(segments, ((place + hop) % parts) * rows, rows)
        for hop in range(parts)
    ]
    seg_rows = seg_blocks[0]
    seg_q = seg_rows[None, :]
    seg_k = jnp.concatenate(seg_blocks)[:, None]
    start = place * rows
    near = jnp.stack([segments[:1], segments[-1:]])
    before = lax.dynamic_slice_in_dim(jnp.concatenate([near[0], segments]), start, rows)
    after_rows = lax.dynamic_slice_in_dim(jnp.concatenate([segments[1:], near[1]]), start, rows)
    position = start + jnp.arange(rows)
    keep = jnp.stack(
        [
            ((position > 0) & (before == seg_rows)).astype(F32),
            ((position < length - 1) & (after_rows == seg_rows)).astype(F32),
        ]
    )[:, :, None]

    keys = dot(token_in, key_low).astype(BF16)
    values = (dot(token_in, value_low) + bias_value).astype(BF16)
    keys_values = jnp.concatenate([keys, values], axis=1)
    keys_values, query_low, onehot, output_proj, expand_proj, shrink_proj, token_proj, char_proj = land(
        [], keys_values, query_low, onehot, output_proj, expand_proj, shrink_proj, token_proj, char_proj
    )
    blocks = [keys_values] + [shift_shard(keys_values, hop) for hop in range(1, parts)]
    queries = (dot(token_in, query_low) + bias_query).astype(BF16)
    up_fetch = Fetch([output_proj, expand_proj], True)
    down_fetch = Fetch([shrink_proj, token_proj, char_proj], True)
    kernel_other, queries = land([gate_fetch, up_fetch, down_fetch], kernel_other, queries)
    gate_fetch.swap()
    if spread:
        kernel_low = jnp.moveaxis(in_order(kernel_piece, kernel_other), 0, 1)
        kernel_low = lax.all_gather(kernel_low, ("pair", "core"), axis=2, tiled=True)
        kernel_low = kernel_low.reshape(merging_kernel.shape[0], 2 * width, 2 * width)
    else:
        kernel_low = gather_shard(merging_kernel)
    embedded = dot(onehot, table_low).astype(BF16).reshape(slots, rows + 2, chars)
    letters = (embedded[:, :rows], embedded[:, 2:], embedded[:, 1 : rows + 1])
    input_low, recur_low = gate_fetch.whole()
    up_fetch.cross()
    starts, pooled_low = gru_forward(
        letters, input_low, recur_low, bias_input, bias_recur, counts, keep
    )
    pooled_low, blocks = land([up_fetch], pooled_low, blocks)
    up_fetch.share()
    down_fetch.cross()
    everyone = jnp.concatenate(blocks, axis=0)
    all_keys, all_values = everyone[:, :width], everyone[:, width:]
    mixed, logsum = attend(queries, all_keys, all_values, seg_q, seg_k, HEAD_DIM)
    (mixed,) = land([up_fetch, down_fetch], mixed)
    up_fetch.swap()
    down_fetch.share()

    output_low, expand_low = up_fetch.whole()
    first_in = widen(token_in) + (dot(mixed, output_low) + bias_output)
    first = layer_norm(first_in, gain_first, shift_first)
    first_low = first.astype(BF16)
    up = dot(first_low, expand_low) + bias_expand
    hidden = gelu_exact(up).astype(BF16)
    (hidden,) = land([down_fetch], hidden)
    down_fetch.swap()
    shrink_low, project_token, project_char = down_fetch.whole()
    token_mid = first + dot(hidden, shrink_low) + bias_shrink
    mid_low = token_mid.astype(BF16)

    tok_side = dot(mid_low, project_token) + bias_token
    char_side = dot(pooled_low, project_char) + bias_char
    joined = jnp.concatenate([tok_side, char_side], axis=1).astype(BF16)
    joined_ext = with_halo(joined)
    merged = (
        bias_merging
        + dot(joined_ext[0:rows], kernel_low[0])
        + dot(joined_ext[1 : rows + 1], kernel_low[1])
        + dot(joined_ext[2 : rows + 2], kernel_low[2])
    )
    act = gelu_exact(merged)
    tok_pre = token_mid + act[:, :width]
    char_pre = widen(char_in) + act[:, width:]
    token_out = layer_norm(tok_pre, gain_token, shift_token).astype(BF16)
    char_out = layer_norm(char_pre, gain_char, shift_char).astype(BF16)

    _, token_pull = jax.vjp(layer_norm, tok_pre, gain_token, shift_token)
    tok_pre_grad, token_gain_grad, token_shift_grad = token_pull(widen(token_cot))
    _, char_pull = jax.vjp(layer_norm, char_pre, gain_char, shift_char)
    char_grad, char_gain_grad, char_shift_grad = char_pull(widen(char_cot))
    act_grad = jnp.concatenate([tok_pre_grad, char_grad], axis=1)
    merged_grad = (act_grad * gelu_slope(merged)).astype(BF16)
    merging_bias_grad = jnp.sum(widen(merged_grad), axis=0)
    exchange = flip(
        jnp.concatenate(
            [joined_ext, jnp.pad(core_half(merged_grad, 1 - core), ((0, 2), (0, 0)))], axis=1
        ),
        1,
    )
    merged_ext = with_halo(merged_grad)
    centre = back_product(merged_grad, kernel_low[1])
    exchange, merged_ext, centre = lax.optimization_barrier((exchange, merged_ext, centre))
    joined_pair = (joined_ext, exchange[:, : 2 * width])
    merged_pair = (core_half(merged_grad, core), exchange[:rows, 2 * width :])
    others = [(place + hop) % parts for hop in range(1, parts)]

    def merging_terms(target):
        sources = columns(joined_pair, target, parts)
        return jnp.concatenate(
            [
                pair_product([item[tap : tap + rows] for item in sources], merged_pair)
                for tap in range(3)
            ],
            axis=0,
        )

    token = jnp.zeros((8, 128), F32)
    merging_flow = Flow([merging_terms(j).astype(BF16) for j in others], merging_terms(place))
    token, (centre, merged_ext) = turn(token, [], [merging_flow], centre, merged_ext)
    joined_grad = (
        back_product(merged_ext[2 : rows + 2], kernel_low[0])
        + centre
        + back_product(merged_ext[0:rows], kernel_low[2])
    )
    tok_side_grad = joined_grad[:, :width].astype(BF16)
    char_side_grad = joined_grad[:, width:].astype(BF16)
    token_bias_grad = jnp.sum(widen(tok_side_grad), axis=0)
    char_bias_grad = jnp.sum(widen(char_side_grad), axis=0)
    pooled_grad = back_product(char_side_grad, project_char)
    mid_grad = tok_pre_grad + back_product(tok_side_grad, project_token)

    shrink_out_grad = mid_grad.astype(BF16)
    shrink_bias_grad = jnp.sum(widen(shrink_out_grad), axis=0)
    hidden_grad = back_product(shrink_out_grad, shrink_low)
    up_grad = (hidden_grad * gelu_slope(up)).astype(BF16)
    expand_bias_grad = jnp.sum(widen(up_grad), axis=0)
    middle_own = jnp.concatenate(
        [
            hidden, first_low, mid_low, pooled_low, shrink_out_grad, up_grad, tok_side_grad,
            char_side_grad,
        ],
        axis=1,
    )
    middle_pair = (middle_own, flip(middle_own, 1))
    first_grad = mid_grad + back_product(up_grad, expand_low)
    _, first_pull = jax.vjp(layer_norm, first_in, gain_first, shift_first)
    first_in_grad, first_gain_grad, first_shift_grad = first_pull(first_grad)
    attn_grad = first_in_grad.astype(BF16)
    output_bias_grad = jnp.sum(widen(attn_grad), axis=0)
    mixed_grad = back_product(attn_grad, output_low).astype(BF16)
    mixed_grad, middle_pair = lax.optimization_barrier((mixed_grad, middle_pair))

    def middle_terms(target, dtype):
        if width // parts == PACK:
            deep = ff // 2 // PACK
            at_first = 2 * deep
            at_mid, at_pooled, at_out, at_up = [at_first + 2 * k for k in range(1, 5)]
            at_tok, at_char = at_up + 2 * deep, at_up + 2 * deep + 2
            left = [target * deep + k for k in range(deep)]
            left += [at_up + core * deep + k for k in range(deep)]
            left += [at_mid + target, at_pooled + target]
            right = [at_out + core] * deep + [at_first + target] * deep
            right += [at_tok + core, at_char + core]
            table = jnp.stack([jnp.stack(left), jnp.stack(right)])
            return block_terms(middle_pair, middle_pair, table, PACK, dtype)
        ends = [ff + width * k for k in range(5)] + [2 * ff + width * k for k in range(4, 7)]
        hiddens, firsts, mids, pools, outs, ups, toks, sides = [
            [item[:, lo:hi] for item in middle_pair] for lo, hi in zip([0] + ends[:-1], ends)
        ]
        outs, ups, toks, sides = [
            [core_half(item, core) for item in pair] for pair in (outs, ups, toks, sides)
        ]
        return pack_rows(
            [
                pair_product(columns(hiddens, target, parts), outs),
                pair_product(ups, columns(firsts, target, parts)),
                pair_product(columns(mids, target, parts), toks),
                pair_product(columns(pools, target, parts), sides),
            ],
            PACK,
            dtype,
        )

    middle_flow = Flow([middle_terms(j, BF16) for j in others], None)
    final = jnp.stack([pooled_grad[:, :hid], pooled_grad[:, hid:]])
    token, (mixed_grad, final) = turn(token, [], [middle_flow], mixed_grad, final)

    queries_grad, *terms = attend_back(
        queries, all_keys, all_values, seg_q, seg_k, mixed_grad, logsum, HEAD_DIM
    )
    token, (final, queries_grad, terms, middle_flow.value) = turn(
        token, [merging_flow], [], final, queries_grad, terms, middle_terms(place, BF16)
    )
    away_terms = [shift_shard(terms[hop], -hop % parts) for hop in range(1, parts)]
    late_own = jnp.concatenate([token_in, mixed, queries_grad, attn_grad], axis=1)
    late_other = flip(late_own, 1)

    own_counts = jnp.stack([counts[2], counts[2]])
    own_grads = gru_backward(
        True, letters[2], letters[2], input_low, recur_low, bias_input, bias_recur, own_counts,
        keep, starts, final,
    )
    token, (own_grads, away_terms, late_other) = turn(
        token, [merging_flow], [], own_grads, away_terms, late_other
    )
    owned = widen(terms[0])
    for item in away_terms:
        owned = owned + widen(item)
    owned = owned.astype(BF16)
    keys_grad, values_grad = owned[0], owned[1]
    owned_other = flip(owned, 1)
    late_pair = (late_own, late_other)

    def late_terms(targets):
        if width // parts == PACK:
            left = jnp.stack([item for j in targets for item in (j, 2 + j)])
            right = jnp.stack([4 + core, 6 + core] * len(targets))
            first = block_terms(late_pair, late_pair, jnp.stack([left, right]), PACK, BF16)
            first, owned_other_now = lax.optimization_barrier((first, owned_other))
            owned_pair = (owned, owned_other_now)
            left = jnp.stack([item for j in targets for item in (j, j)])
            right = jnp.stack([core, 2 + core] * len(targets))
            second = block_terms(late_pair, owned_pair, jnp.stack([left, right]), PACK, BF16)
            deep = 2 * PACK
            return [
                jnp.concatenate([item[k * deep : (k + 1) * deep] for item in (first, second)], axis=0)
                for k in range(len(targets))
            ]
        inputs, mixes, query_part, attn_part = [
            [item[:, k * width : (k + 1) * width] for item in late_pair] for k in range(4)
        ]
        key_part, value_part = [
            [item[k] for item in (owned, owned_other)] for k in range(2)
        ]
        products = (
            (inputs, query_part), (mixes, attn_part), (inputs, key_part), (inputs, value_part)
        )
        return [
            pack_rows(
                [
                    pair_product(columns(one, j, parts), [core_half(item, core) for item in two])
                    for one, two in products
                ],
                PACK,
                BF16,
            )
            for j in targets
        ]

    *late_sent, late_own_terms = late_terms(others + [place])
    late_flow = Flow(late_sent, late_own_terms)
    token, (own_grads,) = turn(token, [], [late_flow], own_grads)

    near_grads = gru_backward(
        False, letters[0], letters[1], input_low, recur_low, bias_input, bias_recur, counts[:2],
        keep, starts, own_grads[2], own_grads[3:],
    )
    token, (own_grads, near_grads) = turn(
        token, [late_flow, merging_flow, middle_flow], [], own_grads, near_grads
    )

    table_grad = table_terms_of(id_columns, *near_grads[:2], *own_grads[:2], vocab)
    query_bias_grad = jnp.sum(widen(queries_grad), axis=0)
    value_bias_grad = jnp.sum(widen(values_grad), axis=0)
    bias_input_grad, bias_recur_grad = near_grads[5:]
    vector_grads = (
        query_bias_grad, value_bias_grad, output_bias_grad, first_gain_grad, first_shift_grad,
        expand_bias_grad, shrink_bias_grad, bias_input_grad[:, 0], bias_recur_grad[:, 0],
        token_bias_grad, char_bias_grad, merging_bias_grad, token_gain_grad, token_shift_grad,
        char_gain_grad, char_shift_grad,
    )
    vector_terms = jnp.concatenate(
        [
            jnp.moveaxis(item.reshape(item.shape[:-1] + (parts, -1)), -2, 0).reshape(parts, -1)
            for item in vector_grads
        ],
        axis=1,
    ).reshape(parts, 2, -1, PACK)
    chars_part, hid_part = chars // parts, hid // parts
    part, joint = width // parts, 2 * width // parts
    tail_rows = vocab // parts // 2
    gru_shapes = [
        (chars_part, gate_width), (hid_part, gate_width), (tail_rows, PACK),
        (vector_terms.shape[2], PACK),
    ]
    depth = sum(deep * lanes for deep, lanes in gru_shapes) // PACK
    depth += -depth % (4 * rep_size())
    table_terms = table_grad.reshape(parts, 2, tail_rows, chars)
    gru_sums = near_grads[3:5]
    gru_away = pack_gru_terms(
        1 - core, gru_sums, table_terms, vector_terms, depth, PACK, BF16
    )
    token, (gru_sums, table_terms, vector_terms, gru_away) = turn(
        token, [late_flow], [], gru_sums, table_terms, vector_terms, gru_away
    )
    gru_away = flip(gru_away, 1)
    gru_own = pack_gru_terms(core, gru_sums, table_terms, vector_terms, depth, PACK, F32)
    token, (gru_own, gru_away) = turn(token, [], [], gru_own, gru_away)
    gru_total = gru_own + widen(gru_away)
    gru_flow = Flow(
        [lax.dynamic_index_in_dim(gru_total, j, 0, keepdims=False).astype(BF16) for j in others],
        lax.dynamic_index_in_dim(gru_total, place, 0, keepdims=False),
    )
    token, (queries_grad, keys_grad, values_grad) = turn(
        token, [], [gru_flow], queries_grad, keys_grad, values_grad
    )
    token_grad = (
        first_in_grad
        + back_product(queries_grad, query_low)
        + back_product(keys_grad, key_low)
        + back_product(values_grad, value_low)
    )
    flows = dict(a=merging_flow, b=middle_flow, c=late_flow, d=gru_flow)
    shapes = dict(
        a=[(3 * joint, width, "lanes")],
        b=[
            (ff // parts, PACK, "lanes"), (ff // 2, part, "turned"), (part, PACK, "lanes"),
            (part, PACK, "lanes"),
        ],
        c=[(part, PACK, "lanes")] * 4,
        d=[
            (chars_part, gate_width, "stacked"), (hid_part, gate_width, "stacked"),
            (tail_rows, chars, "rows"), (vector_terms.shape[2], PACK, "stacked"),
        ],
    )
    for name in TAIL + "abcd" * 16:
        token, _ = turn(token, [flows[name]], [])
    owned_shards = {name: weights_of(flow.value, shapes[name]) for name, flow in flows.items()}
    (merging_out,) = owned_shards["a"]
    merging_out = merging_out.reshape(3, joint, 2 * width)
    shrink_out, expand_out, token_proj_out, char_proj_out = owned_shards["b"]
    query_out, output_out, key_out, value_out = owned_shards["c"]
    input_out, recur_out, table_out, flat_out = owned_shards["d"]
    flat_out = flat_out.reshape(-1)
    vector_out, at = [], 0
    for item in vectors:
        vector_out.append(flat_out[at : at + item.size].reshape(item.shape))
        at += item.size
    (
        query_bias_out, value_bias_out, output_bias_out, first_gain_out, first_shift_out,
        expand_bias_out, shrink_bias_out, input_bias_out, recur_bias_out, token_bias_out,
        char_bias_out, merging_bias_out, token_gain_out, token_shift_out, char_gain_out,
        char_shift_out,
    ) = vector_out
    return (
        token_out, char_out, token_grad, char_grad,
        query_out, key_out, value_out, output_out,
        query_bias_out, value_bias_out, output_bias_out, first_gain_out, first_shift_out,
        expand_out, expand_bias_out, shrink_out, shrink_bias_out, table_out,
        input_out, input_bias_out, recur_out, recur_bias_out,
        token_proj_out, token_bias_out, char_proj_out, char_bias_out,
        merging_out, merging_bias_out, token_gain_out, token_shift_out, char_gain_out,
        char_shift_out,
    )


def solution(mesh):
    sizes = (mesh.shape["rep"] // 2, 2, mesh.shape["shard"])
    mesh = jax.sharding.Mesh(mesh.devices.reshape(sizes), ("pair", "core", "shard"))
    rows = P(("pair", "core", "shard"), None)
    split, vector = P("shard", None), P("shard")
    in_specs = (
        rows, rows, rows, P(("pair", "core", "shard")), P(("pair", "core")), rows, rows,
        split, split, split, split, vector, vector, vector, vector, vector,
        split, vector, split, vector, split,
        P(None, "shard", None), P(None, "shard"), P(None, "shard", None), P(None, "shard"),
        split, vector, split, vector, P(None, "shard", None), vector,
        vector, vector, vector, vector,
    )
    out_specs = (rows,) * 4 + in_specs[7:]
    return jax.shard_map(shards, mesh=mesh, in_specs=in_specs, out_specs=out_specs, check_vma=False)
```

```python
import functools
import jax
import jax.numpy as jnp
from jax import lax
from jax.sharding import PartitionSpec as P
from jax.experimental import pallas as pl
from jax.experimental.pallas import tpu as pltpu

F32 = jnp.float32
BF16 = jnp.bfloat16
VMEM_BYTES = 60 * 1024 * 1024
LIGHT = pl.CostEstimate(flops=1024, bytes_accessed=1024, transcendentals=0)


def dot(left, right):
    return jnp.dot(left, right, preferred_element_type=F32)


def dot_nt(left, right):
    return lax.dot_general(left, right, (((1,), (1,)), ((), ())), preferred_element_type=F32)


def dot_tn(left, right):
    return lax.dot_general(left, right, (((0,), (0,)), ((), ())), preferred_element_type=F32)


def sigmoid(values):
    return 0.5 * jnp.tanh(0.5 * values) + 0.5


def chunks(rows):
    size = min(rows, 512)
    return [slice(start, start + size) for start in range(0, rows, size)]


def gru_specs(slots, rows, chars, gate_width, at):
    hid = gate_width // 3
    whole = lambda *shape: pl.BlockSpec(shape, lambda i: (0,) * len(shape))
    letters = lambda place: pl.BlockSpec((1, rows, chars), lambda i: (place(at(i)), 0, 0))
    last = slots - 1
    return [
        letters(lambda t: jnp.minimum(t, last)),
        letters(lambda t: jnp.maximum(last - t, 0)),
        letters(lambda t: jnp.maximum(t - slots, 0)),
        letters(lambda t: jnp.minimum(2 * slots - 1 - t, last)),
        whole(2, chars, gate_width),
        whole(2, hid, gate_width),
        whole(2, 1, gate_width),
        whole(2, 1, gate_width),
        whole(3, rows, 1),
        whole(2, rows, 1),
    ]


def gru_gates(letter, start_low, wi, wr, bi, br, hid):
    both = 2 * hid
    mixed = dot(letter, wi[:, :both]) + dot(start_low, wr[:, :both]) + (bi[:, :both] + br[:, :both])
    reset = sigmoid(mixed[:, :hid])
    update = sigmoid(mixed[:, hid:])
    carried = dot(start_low, wr[:, both:]) + br[:, both:]
    candidate = jnp.tanh(dot(letter, wi[:, both:]) + bi[:, both:] + reset * carried)
    return reset, update, candidate, carried


def gru_forward_kernel(slots, a0, a1, b0, b1, wi, wr, bi, br, counts, keep, starts, pooled, state):
    step = pl.program_id(0)
    rows, hid = state.shape[1], state.shape[2]

    @pl.when(step == 0)
    def _():
        state[...] = jnp.zeros_like(state)

    @pl.when(step == slots)
    def _():
        for way in range(2):
            state[way] = state[way] * keep[way]

    first = step < slots
    place = jnp.where(first, step, step - slots)
    for part in chunks(rows):
        for way, (near, own) in enumerate(((a0, b0), (a1, b1))):
            letter = jnp.where(first, near[0, part], own[0, part])
            start = state[way, part]
            starts[0, way, part] = start
            _, update, candidate, _ = gate_values = gru_gates(
                letter, start.astype(BF16), wi[way], wr[way], bi[way], br[way], hid
            )
            fresh = candidate + update * (start - candidate)
            slot = place if way == 0 else slots - 1 - place
            count = jnp.where(first, counts[way, part], counts[2, part])
            state[way, part] = jnp.where(slot < count, fresh, start)

    @pl.when(step == 2 * slots - 1)
    def _():
        for way in range(2):
            pooled[:, way * hid : (way + 1) * hid] = state[way].astype(BF16)


def gru_forward(letters, wi, wr, bi, br, counts, keep):
    near0, near1, own = letters
    slots, rows, chars = own.shape
    gate_width = wi.shape[-1]
    hid = gate_width // 3
    return pl.pallas_call(
        functools.partial(gru_forward_kernel, slots),
        grid=(2 * slots,),
        in_specs=gru_specs(slots, rows, chars, gate_width, lambda i: i),
        out_specs=[
            pl.BlockSpec((1, 2, rows, hid), lambda i: (i, 0, 0, 0)),
            pl.BlockSpec((rows, 2 * hid), lambda i: (0, 0)),
        ],
        out_shape=[
            jax.ShapeDtypeStruct((2 * slots, 2, rows, hid), F32),
            jax.ShapeDtypeStruct((rows, 2 * hid), BF16),
        ],
        scratch_shapes=[pltpu.VMEM((2, rows, hid), F32)],
        compiler_params=pltpu.CompilerParams(vmem_limit_bytes=VMEM_BYTES),
        cost_estimate=LIGHT,
        name="gru_forward",
    )(near0, near1, own, own, wi, wr, bi, br, counts, keep)


def gru_backward_kernel(slots, last, x0, x1, wi, wr, bi, br, counts, keep, starts, final, *refs):
    sums, refs = (None, refs) if last else (refs[:4], refs[4:])
    letter_grads, (start_grad, wi_grad, wr_grad, bi_grad, br_grad) = refs[:2], refs[2:]
    back = pl.program_id(0)
    place = slots - 1 - back
    rows, hid = final.shape[1], final.shape[2]
    both = 2 * hid

    @pl.when(back == 0)
    def _():
        start_grad[...] = final[...]
        for k, total in enumerate((wi_grad, wr_grad, bi_grad, br_grad)):
            total[...] = jnp.zeros_like(total) if last else sums[k][...]

    for part in chunks(rows):
        for way, letters in enumerate((x0, x1)):
            letter = letters[0, part]
            start = starts[0, way, part]
            start_low = start.astype(BF16)
            reset, update, candidate, carried = gru_gates(
                letter, start_low, wi[way], wr[way], bi[way], br[way], hid
            )
            slot = place if way == 0 else slots - 1 - place
            grad = start_grad[way, part]
            fresh = jnp.where(slot < counts[way, part], grad, 0.0)
            kept = grad - fresh
            scaled = fresh * (1.0 - update)
            cand_pre = scaled * (1.0 - candidate * candidate)
            update_pre = scaled * update * (start - candidate)
            cand_reset = cand_pre * reset
            reset_pre = cand_reset * carried * (1.0 - reset)
            shared = jnp.concatenate([reset_pre.astype(BF16), update_pre.astype(BF16)], axis=1)
            cand_in = cand_pre.astype(BF16)
            cand_rec = cand_reset.astype(BF16)
            start_grad[way, part] = (
                kept
                + update * fresh
                + dot_nt(shared, wr[way, :, :both])
                + dot_nt(cand_rec, wr[way, :, both:])
            )
            letter_grads[way][0, part] = (
                dot_nt(shared, wi[way, :, :both]) + dot_nt(cand_in, wi[way, :, both:])
            ).astype(BF16)
            wi_grad[way, :, :both] += dot_tn(letter, shared)
            wi_grad[way, :, both:] += dot_tn(letter, cand_in)
            wr_grad[way, :, :both] += dot_tn(start_low, shared)
            wr_grad[way, :, both:] += dot_tn(start_low, cand_rec)
            total = jnp.sum(shared.astype(F32), axis=0, keepdims=True)
            bi_grad[way, :, :both] += total
            br_grad[way, :, :both] += total
            bi_grad[way, :, both:] += jnp.sum(cand_in.astype(F32), axis=0, keepdims=True)
            br_grad[way, :, both:] += jnp.sum(cand_rec.astype(F32), axis=0, keepdims=True)

    if last:

        @pl.when(back == slots - 1)
        def _():
            for way in range(2):
                start_grad[way] = start_grad[way] * keep[way]


def gru_backward(last, near0, near1, wi, wr, bi, br, counts, keep, starts, final, sums=()):
    slots, rows, chars = near0.shape
    gate_width = wi.shape[-1]
    hid = gate_width // 3
    offset = slots if last else 0
    whole = lambda *shape: pl.BlockSpec(shape, lambda i: (0,) * len(shape))
    return pl.pallas_call(
        functools.partial(gru_backward_kernel, slots, last),
        grid=(slots,),
        in_specs=[
            pl.BlockSpec((1, rows, chars), lambda i: (slots - 1 - i, 0, 0)),
            pl.BlockSpec((1, rows, chars), lambda i: (i, 0, 0)),
            whole(2, chars, gate_width),
            whole(2, hid, gate_width),
            whole(2, 1, gate_width),
            whole(2, 1, gate_width),
            whole(2, rows, 1),
            whole(2, rows, 1),
            pl.BlockSpec((1, 2, rows, hid), lambda i: (offset + slots - 1 - i, 0, 0, 0)),
            whole(2, rows, hid),
        ]
        + [whole(*item.shape) for item in sums],
        out_specs=[
            pl.BlockSpec((1, rows, chars), lambda i: (slots - 1 - i, 0, 0)),
            pl.BlockSpec((1, rows, chars), lambda i: (i, 0, 0)),
            whole(2, rows, hid),
            whole(2, chars, gate_width),
            whole(2, hid, gate_width),
            whole(2, 1, gate_width),
            whole(2, 1, gate_width),
        ],
        out_shape=[
            jax.ShapeDtypeStruct((slots, rows, chars), BF16),
            jax.ShapeDtypeStruct((slots, rows, chars), BF16),
            jax.ShapeDtypeStruct((2, rows, hid), F32),
            jax.ShapeDtypeStruct((2, chars, gate_width), F32),
            jax.ShapeDtypeStruct((2, hid, gate_width), F32),
            jax.ShapeDtypeStruct((2, 1, gate_width), F32),
            jax.ShapeDtypeStruct((2, 1, gate_width), F32),
        ],
        compiler_params=pltpu.CompilerParams(vmem_limit_bytes=VMEM_BYTES),
        cost_estimate=LIGHT,
        name="gru_backward",
    )(near0, near1, wi, wr, bi, br, counts, keep, starts, final, *sums)


def half_spec(item, place):
    if item.ndim == 3:
        return pl.BlockSpec((1,) + item.shape[1:], lambda i, w: (place(i, w)[0], place(i, w)[1], 0))
    rows, lanes = item.shape
    return pl.BlockSpec((rows, lanes // 2), lambda i, w: (place(i, w)[1], place(i, w)[0]))


def flat2(ref):
    return ref.at[0] if len(ref.shape) == 3 else ref


def pack_kernel(width, where, *refs):
    out, at = refs[-1], 0
    for ref in refs[:-1]:
        item = flat2(ref)
        rows, lanes = item.shape
        for lane in range(0, lanes, width):
            out[at : at + rows, :] = item[:, lane : lane + width].astype(BF16)
            at += rows


def pack_halves(core, masters, width):
    total = sum(item.size for item in masters) // 2 // width
    where = jnp.stack([core, core])
    return pl.pallas_call(
        functools.partial(pack_kernel, width),
        grid_spec=pltpu.PrefetchScalarGridSpec(
            num_scalar_prefetch=1,
            grid=(1,),
            in_specs=[half_spec(item, lambda i, w: (w[0], 0)) for item in masters],
            out_specs=pl.BlockSpec((total, width), lambda i, w: (0, 0)),
        ),
        out_shape=jax.ShapeDtypeStruct((total, width), BF16),
        compiler_params=pltpu.CompilerParams(vmem_limit_bytes=VMEM_BYTES),
        cost_estimate=LIGHT,
        name="pack_halves",
    )(where, *masters)


def table_kernel(ids, near0, near1, own0, own1, out):
    @pl.when(pl.program_id(0) == 0)
    def _():
        out[...] = jnp.zeros_like(out)

    own = (own0[0].astype(F32) + own1[0].astype(F32)).astype(BF16)
    rows, vocab = own.shape[0], out.shape[0]
    letters = lax.broadcasted_iota(jnp.int32, (rows, vocab), 1)
    total = None
    for which, grad in enumerate((near0[0], near1[0], own)):
        chosen = jnp.where(ids[which, 0] == letters, 1.0, 0.0).astype(BF16)
        part = dot_tn(chosen, grad)
        total = part if total is None else total + part
    out[...] += total


def table_terms_of(ids, near0, near1, own0, own1, vocab):
    slots, rows, chars = near0.shape
    one = pl.BlockSpec((1, rows, chars), lambda i: (i, 0, 0))
    return pl.pallas_call(
        table_kernel,
        grid=(slots,),
        in_specs=[pl.BlockSpec((3, 1, rows, 1), lambda i: (0, i, 0, 0)), one, one, one, one],
        out_specs=pl.BlockSpec((vocab, chars), lambda i: (0, 0)),
        out_shape=jax.ShapeDtypeStruct((vocab, chars), F32),
        compiler_params=pltpu.CompilerParams(vmem_limit_bytes=VMEM_BYTES),
        cost_estimate=LIGHT,
        name="table_terms",
    )(ids, near0, near1, own0, own1)


def block_terms_kernel(table, a0, b0, a1, b1, out):
    out[...] = (dot_tn(a0[...], b0[...]) + dot_tn(a1[...], b1[...])).astype(out.dtype)


def block_terms(left, right, table, width, dtype):
    rows, count = left[0].shape[0], table.shape[1]
    one = pl.BlockSpec((rows, width), lambda i, t: (0, t[0, i]))
    if right[0].ndim == 3:
        across = right[0].shape[2] // width
        two = pl.BlockSpec(
            (None, rows, width), lambda i, t: (t[1, i] // across, 0, t[1, i] % across)
        )
    else:
        two = pl.BlockSpec((rows, width), lambda i, t: (0, t[1, i]))
    return pl.pallas_call(
        block_terms_kernel,
        grid_spec=pltpu.PrefetchScalarGridSpec(
            num_scalar_prefetch=1,
            grid=(count,),
            in_specs=[one, two, one, two],
            out_specs=pl.BlockSpec((width, width), lambda i, t: (i, 0)),
        ),
        out_shape=jax.ShapeDtypeStruct((count * width, width), dtype),
        compiler_params=pltpu.CompilerParams(vmem_limit_bytes=VMEM_BYTES),
        cost_estimate=LIGHT,
        name="block_terms",
    )(table, left[0], right[0], left[1], right[1])


def unpack_kernel(shapes, where, mine, other, *outs):
    width = mine.shape[1]
    for turn, source in ((0, mine), (1, other)):

        @pl.when(pl.program_id(0) == turn)
        def _(source=source):
            at = 0
            for (rows, lanes, kind), out in zip(shapes, outs):
                if kind == "turned":
                    out[...] = source[at : at + rows, :].astype(F32).T
                    at += rows
                    continue
                target = out.at[0] if kind == "stacked" else out
                for lane in range(0, lanes, width):
                    some = min(width, lanes - lane)
                    target[:, lane : lane + some] = source[at : at + rows, :some].astype(F32)
                    at += rows


def unpack_halves(core, mine, other, shapes):
    where = jnp.stack([core, core])
    half = lambda i, w: jnp.where(i == 0, w[0], 1 - w[0])
    specs, outs = [], []
    for rows, lanes, kind in shapes:
        if kind == "lanes":
            specs.append(pl.BlockSpec((rows, lanes), lambda i, w: (0, half(i, w))))
            outs.append((rows, 2 * lanes))
        elif kind == "stacked":
            specs.append(pl.BlockSpec((1, rows, lanes), lambda i, w: (half(i, w), 0, 0)))
            outs.append((2, rows, lanes))
        elif kind == "rows":
            specs.append(pl.BlockSpec((rows, lanes), lambda i, w: (half(i, w), 0)))
            outs.append((2 * rows, lanes))
        else:
            specs.append(pl.BlockSpec((lanes, rows), lambda i, w: (0, half(i, w))))
            outs.append((lanes, 2 * rows))
    whole = pl.BlockSpec(mine.shape, lambda i, w: (0, 0))
    return pl.pallas_call(
        functools.partial(unpack_kernel, shapes),
        grid_spec=pltpu.PrefetchScalarGridSpec(
            num_scalar_prefetch=1, grid=(2,), in_specs=[whole, whole], out_specs=specs
        ),
        out_shape=[jax.ShapeDtypeStruct(item, F32) for item in outs],
        compiler_params=pltpu.CompilerParams(vmem_limit_bytes=VMEM_BYTES),
        cost_estimate=LIGHT,
        name="unpack_halves",
    )(where, mine, other)


def rows_kernel(width, *refs):
    out, at = refs[-1], 0
    for ref in refs[:-1]:
        rows, lanes = ref.shape
        for lane in range(0, lanes, width):
            out[at : at + rows, :] = ref[:, lane : lane + width].astype(out.dtype)
            at += rows


def pack_rows(blocks, width, dtype):
    blocks = [item if item.shape[1] % width == 0 else item.reshape(-1, width) for item in blocks]
    total = sum(item.size for item in blocks) // width
    return pl.pallas_call(
        functools.partial(rows_kernel, width),
        out_shape=jax.ShapeDtypeStruct((total, width), dtype),
        compiler_params=pltpu.CompilerParams(vmem_limit_bytes=VMEM_BYTES),
        cost_estimate=LIGHT,
        name="pack_rows",
    )(*blocks)


def gru_terms_kernel(width, where, *refs):
    out = refs[-1]
    sums, table, vectors = refs[:-3], refs[-3], refs[-2]
    parts = out.shape[0]
    out[...] = jnp.zeros_like(out)
    for part in range(parts):
        at = 0
        for item in sums:
            rows = item.shape[1] // parts
            rest = slice(part * rows, (part + 1) * rows)
            for lane in range(0, item.shape[2], width):
                out[part, at : at + rows, :] = item[0, rest, lane : lane + width].astype(out.dtype)
                at += rows
        rows, lanes = table.shape[2], table.shape[3]
        out[part, at : at + rows, :lanes] = table[part, 0].astype(out.dtype)
        at += rows
        rows = vectors.shape[2]
        out[part, at : at + rows, :] = vectors[part, 0].astype(out.dtype)


def pack_gru_terms(which, sums, table, vectors, depth, width, dtype):
    parts = table.shape[0]
    where = jnp.stack([which, which])
    chosen = lambda item: pl.BlockSpec((1,) + item.shape[1:], lambda i, w: (w[0], 0, 0))
    second = lambda item: pl.BlockSpec(
        (parts, 1) + item.shape[2:], lambda i, w: (0, w[0], 0, 0)
    )
    return pl.pallas_call(
        functools.partial(gru_terms_kernel, width),
        grid_spec=pltpu.PrefetchScalarGridSpec(
            num_scalar_prefetch=1,
            grid=(1,),
            in_specs=[chosen(item) for item in sums] + [second(table), second(vectors)],
            out_specs=pl.BlockSpec((parts, depth, width), lambda i, w: (0, 0, 0)),
        ),
        out_shape=jax.ShapeDtypeStruct((parts, depth, width), dtype),
        compiler_params=pltpu.CompilerParams(vmem_limit_bytes=VMEM_BYTES),
        cost_estimate=LIGHT,
        name="pack_gru_terms",
    )(where, *sums, table, vectors)


def join_kernel(width, count, where, *refs):
    step = pl.program_id(0)
    masters, (mine, peer), outs = refs[:count], refs[count : count + 2], refs[count + 2 :]

    @pl.when(step < 2)
    def _():
        for master, out in zip(masters, outs):
            out[...] = master[...].astype(BF16)

    for turn, source in ((2, mine), (3, peer)):

        @pl.when(step == turn)
        def _(source=source):
            at = 0
            for out in outs:
                item = flat2(out)
                rows, lanes = item.shape
                for lane in range(0, lanes, width):
                    item[:, lane : lane + width] = source[at : at + rows, :]
                    at += rows


def join_halves(place, core, masters, mine, peer, width):
    where = jnp.stack([place, core])

    def source(i, w):
        return (jnp.minimum(i, 1), 0)

    def target(i, w):
        half = jnp.where(i < 2, i, jnp.where(i == 2, w[1], 1 - w[1]))
        return (half, jnp.where(i < 2, w[0], 1 - w[0]))

    def wide(item):
        return item.shape[:-2] + (2 * item.shape[-2], item.shape[-1])

    rows = pl.BlockSpec(mine.shape, lambda i, w: (0, 0))
    return pl.pallas_call(
        functools.partial(join_kernel, width, len(masters)),
        grid_spec=pltpu.PrefetchScalarGridSpec(
            num_scalar_prefetch=1,
            grid=(4,),
            in_specs=[half_spec(item, source) for item in masters] + [rows, rows],
            out_specs=[half_spec(item, target) for item in masters],
        ),
        out_shape=[jax.ShapeDtypeStruct(wide(item), BF16) for item in masters],
        compiler_params=pltpu.CompilerParams(vmem_limit_bytes=VMEM_BYTES),
        cost_estimate=LIGHT,
        name="join_halves",
    )(where, *masters, mine, peer)


def attend_kernel(scale, q, k, v, seg_q, seg_k, out, logsum):
    pair = q.shape[1]
    half = pair // 2
    allowed = seg_k[...] == seg_q[...]
    lane = lax.broadcasted_iota(jnp.int32, (1, pair), 1)
    keys = k[...]
    values = v[...].T
    for head in range(2):
        mine = (lane < half) if head == 0 else (lane >= half)
        query = jnp.where(mine, q[...] * scale, 0).astype(BF16)
        scores = jnp.where(allowed, dot_nt(keys, query), -1e9)
        top = jnp.max(scores, axis=0, keepdims=True)
        expo = jnp.exp(scores - top)
        total = jnp.sum(expo, axis=0, keepdims=True)
        probs = (expo * (1.0 / total)).astype(BF16)
        logsum[0, head : head + 1, :] = top + jnp.log(total)
        mixed = dot(values[head * half : (head + 1) * half], probs)
        out[:, head * half : (head + 1) * half] = mixed.T.astype(BF16)


def attend(q, k, v, seg_q, seg_k, head_dim):
    rows, width = q.shape
    length = k.shape[0]
    pair = 2 * head_dim
    pairs = width // pair
    return pl.pallas_call(
        functools.partial(attend_kernel, head_dim ** -0.5),
        grid=(pairs,),
        in_specs=[
            pl.BlockSpec((rows, pair), lambda i: (0, i)),
            pl.BlockSpec((length, pair), lambda i: (0, i)),
            pl.BlockSpec((length, pair), lambda i: (0, i)),
            pl.BlockSpec((1, rows), lambda i: (0, 0)),
            pl.BlockSpec((length, 1), lambda i: (0, 0)),
        ],
        out_specs=[
            pl.BlockSpec((rows, pair), lambda i: (0, i)),
            pl.BlockSpec((1, 2, rows), lambda i: (i, 0, 0)),
        ],
        out_shape=[
            jax.ShapeDtypeStruct((rows, width), BF16),
            jax.ShapeDtypeStruct((pairs, 2, rows), F32),
        ],
        compiler_params=pltpu.CompilerParams(vmem_limit_bytes=VMEM_BYTES),
        cost_estimate=LIGHT,
        name="attend",
    )(q, k, v, seg_q, seg_k)


def attend_back_kernel(scale, q, k, v, seg_q, seg_k, grad, logsum, dq, *terms):
    pair = q.shape[1]
    half = pair // 2
    allowed = seg_k[...] == seg_q[...]
    lane = lax.broadcasted_iota(jnp.int32, (1, pair), 1)
    keys = k[...]
    values = v[...]
    keys_t = keys.T
    key_total = None
    value_total = None
    for head in range(2):
        mine = (lane < half) if head == 0 else (lane >= half)
        query = jnp.where(mine, q[...] * scale, 0).astype(BF16)
        out_grad = jnp.where(mine, grad[...], 0).astype(BF16)
        scores = jnp.where(allowed, dot_nt(keys, query), -1e9)
        probs = jnp.exp(scores - logsum[0, head : head + 1, :])
        probs_grad = dot_nt(values, out_grad)
        delta = jnp.sum(probs * probs_grad, axis=0, keepdims=True)
        scores_grad = (probs * (probs_grad - delta)).astype(BF16)
        key_part = dot(scores_grad, query)
        value_part = dot(probs.astype(BF16), out_grad)
        key_total = key_part if head == 0 else key_total + key_part
        value_total = value_part if head == 0 else value_total + value_part
        query_part = dot(keys_t[head * half : (head + 1) * half], scores_grad)
        dq[:, head * half : (head + 1) * half] = (query_part.T * scale).astype(BF16)
    for part, out in enumerate(terms):
        rows = slice(part * out.shape[1], (part + 1) * out.shape[1])
        out[0] = key_total[rows].astype(BF16)
        out[1] = value_total[rows].astype(BF16)


def attend_back(q, k, v, seg_q, seg_k, grad, logsum, head_dim):
    rows, width = q.shape
    length = k.shape[0]
    pair = 2 * head_dim
    pairs = width // pair
    return pl.pallas_call(
        functools.partial(attend_back_kernel, head_dim ** -0.5),
        grid=(pairs,),
        in_specs=[
            pl.BlockSpec((rows, pair), lambda i: (0, i)),
            pl.BlockSpec((length, pair), lambda i: (0, i)),
            pl.BlockSpec((length, pair), lambda i: (0, i)),
            pl.BlockSpec((1, rows), lambda i: (0, 0)),
            pl.BlockSpec((length, 1), lambda i: (0, 0)),
            pl.BlockSpec((rows, pair), lambda i: (0, i)),
            pl.BlockSpec((1, 2, rows), lambda i: (i, 0, 0)),
        ],
        out_specs=[
            pl.BlockSpec((rows, pair), lambda i: (0, i)),
        ]
        + [pl.BlockSpec((2, rows, pair), lambda i: (0, 0, i))] * (length // rows),
        out_shape=[jax.ShapeDtypeStruct((rows, width), BF16)]
        + [jax.ShapeDtypeStruct((2, rows, width), BF16)] * (length // rows),
        compiler_params=pltpu.CompilerParams(vmem_limit_bytes=VMEM_BYTES),
        cost_estimate=LIGHT,
        name="attend_back",
    )(q, k, v, seg_q, seg_k, grad, logsum)


HEAD_DIM = 64
PACK = 384
TAIL = "adbcdacdbcdabcdbdb"
norm_eps = 1e-05


def layer_norm(values, gain, shift):
    centre = jnp.mean(values, axis=-1, keepdims=True)
    centred = values - centre
    spread = jnp.mean(centred * centred, axis=-1, keepdims=True)
    return centred * lax.rsqrt(spread + norm_eps) * gain + shift


ERFC = (
    -1.26551223, 1.00002368, 0.37409196, 0.09678418, -0.18628806, 0.27886807, -1.13520398,
    1.48851587, -0.82215223, 0.17087277,
)


def normal_share(values):
    size = jnp.abs(values) * (0.5 ** 0.5)
    place = 1.0 / (1.0 + 0.5 * size)
    power = ERFC[-1]
    for term in ERFC[-2::-1]:
        power = power * place + term
    tail = 0.5 * place * jnp.exp(power - size * size)
    return jnp.where(values < 0, tail, 1.0 - tail)


def gelu_exact(values):
    return values * normal_share(values)


def gelu_slope(values):
    return normal_share(values) + values * jnp.exp(-0.5 * values * values) * 0.3989422804014327


def widen(values):
    return values.astype(F32)


def back_product(grad, weight):
    return jnp.einsum("rg,cg->rc", grad, weight, preferred_element_type=F32)


def rep_size():
    return 2 * lax.axis_size("pair")


def rep_index():
    return 2 * lax.axis_index("pair") + lax.axis_index("core")


def flip(value, bit):
    if bit == 1:
        return lax.ppermute(value, "core", [(0, 1), (1, 0)])
    count = lax.axis_size("pair")
    return lax.ppermute(value, "pair", [(i, i ^ (bit // 2)) for i in range(count)])


def shift_shard(value, hop):
    count = lax.axis_size("shard")
    return lax.ppermute(value, "shard", [(i, (i - hop) % count) for i in range(count)])


def neighbour_rows(first, last):
    count, place = lax.axis_size("shard"), lax.axis_index("shard")
    if count == 2:
        got = lax.ppermute(jnp.where(place == 0, last, first), "shard", [(0, 1), (1, 0)])
        nothing = jnp.zeros_like(got)
        return jnp.where(place == 0, nothing, got), jnp.where(place == 0, got, nothing)
    up = [(i, i + 1) for i in range(count - 1)]
    down = [(i + 1, i) for i in range(count - 1)]
    return lax.ppermute(last, "shard", up), lax.ppermute(first, "shard", down)


def with_halo(value):
    before, after = neighbour_rows(value[:1], value[-1:])
    return jnp.concatenate([before, value, after], axis=0)


def small_pieces(masters):
    fits = all(item.shape[-2] % (8 * rep_size()) == 0 for item in masters)
    return fits and lax.axis_size("shard") == 2


def own_piece(master):
    rows = master.shape[-2] // rep_size()
    return lax.dynamic_slice_in_dim(master, rep_index() * rows, rows, master.ndim - 2).astype(BF16)


def in_order(piece, other):
    first = lax.axis_index("shard") == 0
    return jnp.stack([jnp.where(first, piece, other), jnp.where(first, other, piece)])


def gather_shard(master):
    return lax.all_gather(master.astype(BF16), "shard", axis=master.ndim - 2, tiled=True)


class Fetch:
    def __init__(self, masters, spread=False):
        self.masters = masters
        self.alone = lax.axis_size("shard") != 2
        self.spread = spread and rep_size() > 2
        self.core = rep_index() % 2
        self.side = rep_index() // 2 % 2
        if self.alone:
            self.state = [gather_shard(item) for item in masters]
            return
        self.state = pack_halves(self.core, masters, PACK)
        if self.spread:
            half = self.state.shape[0] // 2
            self.state = lax.dynamic_slice_in_dim(self.state, self.side * half, half, 0)

    def cross(self):
        if not self.alone:
            self.state = shift_shard(self.state, 1)

    def share(self):
        if not self.alone and self.spread:
            self.state = (self.state, flip(self.state, 2))

    def swap(self):
        if self.alone:
            return
        if self.spread:
            mine, other = self.state
            self.state = jnp.concatenate(
                [
                    jnp.where(self.side == 0, mine, other),
                    jnp.where(self.side == 0, other, mine),
                ],
                axis=0,
            )
        self.state = (self.state, flip(self.state, 1))

    def whole(self):
        if self.alone:
            return self.state
        place = lax.axis_index("shard")
        return join_halves(place, self.core, self.masters, *self.state, PACK)


def land(fetches, *values):
    states, values = lax.optimization_barrier(([item.state for item in fetches], values))
    for item, state in zip(fetches, states):
        item.state = state
    return values


def gather_small(value):
    if lax.axis_size("shard") != 2:
        return lax.all_gather(value, "shard")
    place = lax.axis_index("shard")
    other = lax.ppermute(value, "shard", [(0, 1), (1, 0)])
    return jnp.stack([jnp.where(place == 0, value, other), jnp.where(place == 0, other, value)])


def both_cores(*values):
    widths = [value.shape[1] for value in values]
    other = flip(jnp.concatenate(values, axis=1), 1)
    result, at = [], 0
    for value, width in zip(values, widths):
        result.append((value, other[:, at : at + width]))
        at += width
    return result


def core_half(value, which):
    half = value.shape[1] // 2
    return lax.dynamic_slice_in_dim(value, which * half, half, 1)


def pair_product(left, right):
    total = None
    for one, two in zip(left, right):
        part = jnp.einsum("rc,rg->cg", one, two, preferred_element_type=F32)
        total = part if total is None else total + part
    return total


def columns(pair, place, parts):
    size = pair[0].shape[1] // parts
    return [lax.dynamic_slice_in_dim(item, place * size, size, 1) for item in pair]


def weights_of(pair, shapes):
    core, width = lax.axis_index("core"), pair[0].shape[1]
    if all(lanes % width == 0 or kind == "rows" for _, lanes, kind in shapes):
        return unpack_halves(core, *pair, shapes)
    low, high = [jnp.where(core == k, pair[0], pair[1]) for k in range(2)]
    blocks, at = [], 0
    for rows, lanes, kind in shapes:
        if kind == "rows":
            halves = [half[at : at + rows, :lanes] for half in (low, high)]
            at += rows
        elif lanes % width:
            size = rows * lanes // width
            halves = [half[at : at + size].reshape(rows, lanes) for half in (low, high)]
            at += size
        else:
            count = lanes // width
            halves = [
                jnp.concatenate(
                    [half[at + k * rows : at + (k + 1) * rows] for k in range(count)], axis=1
                )
                for half in (low, high)
            ]
            at += count * rows
        halves = [widen(half) for half in halves]
        if kind == "stacked":
            blocks.append(jnp.stack(halves))
        elif kind == "turned":
            blocks.append(jnp.concatenate(halves, axis=0).T)
        else:
            blocks.append(jnp.concatenate(halves, axis=1 if kind == "lanes" else 0))
    return blocks


class Flow:
    def __init__(self, sent, value):
        self.value, self.away = value, sent
        bits = [1 << k for k in range(1, (rep_size() - 1).bit_length())]
        self.stages = [("shard", 0)] + [("halve", bit) for bit in bits]
        self.stages += [("double", bit) for bit in bits[::-1]] + [("core", 1)]
        if len(bits) > 1:
            self.stages[2:-2] = [("scatter", 0), ("gather", 0)]

    def launch(self):
        kind, bit = self.stages[0]
        if kind == "shard":
            parts = lax.axis_size("shard")
            self.got = [shift_shard(item, -hop % parts) for hop, item in enumerate(self.away, 1)]
        elif kind in ("scatter", "gather"):
            self.got = [flip(item, 4 * hop) for hop, item in enumerate(self.away, 1)]
        else:
            self.got = [flip(item, bit) for item in self.away]

    @staticmethod
    def by_place(items):
        whole, z = jnp.stack(items), rep_index() // 4
        return [
            lax.dynamic_index_in_dim(whole, jnp.bitwise_xor(z, p), 0, keepdims=False)
            for p in range(len(items))
        ]

    def combine(self):
        kind, bit = self.stages.pop(0)
        side = (rep_index() // max(bit, 1)) % 2
        if kind in ("shard", "halve", "scatter"):
            total = widen(self.value)
            for item in self.got:
                total = total + widen(item)
            self.value = total.astype(BF16)
        elif kind == "core":
            self.value = (self.value, self.got[0])
        elif kind == "gather":
            self.value = jnp.concatenate(self.by_place([self.value] + self.got), axis=0)
        else:
            low = jnp.where(side == 0, self.value, self.got[0])
            high = jnp.where(side == 0, self.got[0], self.value)
            self.value = jnp.concatenate([low, high], axis=0)
        if not self.stages:
            return
        kind, bit = self.stages[0]
        if kind in ("scatter", "gather"):
            count = rep_size() // 4
            self.away = [self.value] * (count - 1)
            if kind == "scatter":
                rows = self.value.shape[0] // count
                self.value, *self.away = self.by_place(
                    [self.value[k * rows : (k + 1) * rows] for k in range(count)]
                )
        elif kind == "halve":
            half = self.value.shape[0] // 2
            side = (rep_index() // bit) % 2
            self.away = [lax.dynamic_slice_in_dim(self.value, (1 - side) * half, half, 0)]
            self.value = lax.dynamic_slice_in_dim(self.value, side * half, half, 0)
        else:
            self.away = [self.value]


def turn(token, landing, starting, *values):
    landing = [flow for flow in landing if flow.stages]
    got, values, token = lax.optimization_barrier(([flow.got for flow in landing], values, token))
    for flow, item in zip(landing, got):
        flow.got = item
        flow.combine()
    going = [flow for flow in landing if flow.stages] + list(starting)
    away, values, token = lax.optimization_barrier(([flow.away for flow in going], values, token))
    for flow, item in zip(going, away):
        flow.away = item
        flow.launch()
    return token, values


def shards(
    token_in,
    char_in,
    char_ids,
    char_counts,
    segments,
    token_cot,
    char_cot,
    query_proj,
    key_proj,
    value_proj,
    output_proj,
    query_bias,
    value_bias,
    output_bias,
    first_gain,
    first_shift,
    expand_proj,
    expand_bias,
    shrink_proj,
    shrink_bias,
    char_table,
    gate_input,
    input_bias,
    gate_recur,
    recur_bias,
    token_proj,
    token_bias,
    char_proj,
    char_bias,
    merging_kernel,
    merging_bias,
    token_gain,
    token_shift,
    char_gain,
    char_shift,
):
    rows, width = token_in.shape
    place, parts = lax.axis_index("shard"), lax.axis_size("shard")
    rep = rep_index()
    core = rep % 2
    slots = char_ids.shape[1]
    chars = char_table.shape[1]
    vocab = char_table.shape[0] * parts
    gate_width = gate_input.shape[-1]
    hid = gate_width // 3
    ff = expand_proj.shape[1]

    first_fetch = Fetch([query_proj, key_proj, value_proj])
    gate_input, gate_recur, merging_kernel, flat_first = land(
        [first_fetch], gate_input, gate_recur, merging_kernel, query_bias
    )
    first_fetch.cross()
    spread = small_pieces([merging_kernel])
    kernel_piece = own_piece(merging_kernel) if spread else jnp.zeros((8, 128), BF16)
    gate_fetch = Fetch([gate_input, gate_recur])

    vectors = (
        flat_first, value_bias, output_bias, first_gain, first_shift, expand_bias, shrink_bias,
        input_bias, recur_bias, token_bias, char_bias, merging_bias, token_gain, token_shift,
        char_gain, char_shift,
    )
    flat = jnp.concatenate([item.reshape(-1) for item in vectors]).astype(BF16)
    pad = -flat.shape[0] % (8 * chars)
    small = jnp.concatenate(
        [char_table.astype(BF16), jnp.pad(flat, (0, pad)).reshape(-1, chars)], axis=0
    )
    packed_ids = jnp.concatenate([char_ids, char_counts[:, None]], axis=1)
    small, packed_ids, kernel_piece = land([first_fetch, gate_fetch], small, packed_ids, kernel_piece)
    gate_fetch.cross()
    first_fetch.swap()
    kernel_other = shift_shard(kernel_piece, 1) if spread else kernel_piece
    small = gather_small(small)
    ids_ext = with_halo(packed_ids)
    query_low, key_low, value_low = first_fetch.whole()
    table_low = small[:, : char_table.shape[0]].reshape(vocab, chars)
    tail = widen(small[:, char_table.shape[0] :].reshape(parts, -1))
    wide, at = [], 0
    for item in vectors:
        size = item.size
        block = tail[:, at : at + size].reshape((parts,) + item.shape)
        at += size
        if item.ndim == 2:
            wide.append(block.transpose(1, 0, 2).reshape(item.shape[0], 1, -1))
        else:
            wide.append(block.reshape(-1))
    (
        bias_query, bias_value, bias_output, gain_first, shift_first, bias_expand, bias_shrink,
        bias_input, bias_recur, bias_token, bias_char, bias_merging, gain_token, shift_token,
        gain_char, shift_char,
    ) = wide

    counts_ext = ids_ext[:, slots]
    onehot = (
        ids_ext[:, :slots].T.reshape(-1)[:, None] == jnp.arange(vocab, dtype=jnp.int32)[None, :]
    ).astype(BF16)
    letters_of = [ids_ext[at : at + rows, :slots].T for at in (0, 2, 1)]
    id_columns = jnp.stack(letters_of)[..., None]
    counts = jnp.stack([counts_ext[:rows], counts_ext[2:], counts_ext[1 : rows + 1]])[:, :, None]
    length = segments.shape[0]
    seg_blocks = [
        lax.dynamic_slice_in_dim(segments, ((place + hop) % parts) * rows, rows)
        for hop in range(parts)
    ]
    seg_rows = seg_blocks[0]
    seg_q = seg_rows[None, :]
    seg_k = jnp.concatenate(seg_blocks)[:, None]
    start = place * rows
    near = jnp.stack([segments[:1], segments[-1:]])
    before = lax.dynamic_slice_in_dim(jnp.concatenate([near[0], segments]), start, rows)
    after_rows = lax.dynamic_slice_in_dim(jnp.concatenate([segments[1:], near[1]]), start, rows)
    position = start + jnp.arange(rows)
    keep = jnp.stack(
        [
            ((position > 0) & (before == seg_rows)).astype(F32),
            ((position < length - 1) & (after_rows == seg_rows)).astype(F32),
        ]
    )[:, :, None]

    keys = dot(token_in, key_low).astype(BF16)
    values = (dot(token_in, value_low) + bias_value).astype(BF16)
    keys_values = jnp.concatenate([keys, values], axis=1)
    keys_values, query_low, onehot, output_proj, expand_proj, shrink_proj, token_proj, char_proj = land(
        [], keys_values, query_low, onehot, output_proj, expand_proj, shrink_proj, token_proj, char_proj
    )
    blocks = [keys_values] + [shift_shard(keys_values, hop) for hop in range(1, parts)]
    queries = (dot(token_in, query_low) + bias_query).astype(BF16)
    up_fetch = Fetch([output_proj, expand_proj], True)
    down_fetch = Fetch([shrink_proj, token_proj, char_proj], True)
    kernel_other, queries = land([gate_fetch, up_fetch, down_fetch], kernel_other, queries)
    gate_fetch.swap()
    if spread:
        kernel_low = jnp.moveaxis(in_order(kernel_piece, kernel_other), 0, 1)
        kernel_low = lax.all_gather(kernel_low, ("pair", "core"), axis=2, tiled=True)
        kernel_low = kernel_low.reshape(merging_kernel.shape[0], 2 * width, 2 * width)
    else:
        kernel_low = gather_shard(merging_kernel)
    embedded = dot(onehot, table_low).astype(BF16).reshape(slots, rows + 2, chars)
    letters = (embedded[:, :rows], embedded[:, 2:], embedded[:, 1 : rows + 1])
    input_low, recur_low = gate_fetch.whole()
    up_fetch.cross()
    starts, pooled_low = gru_forward(
        letters, input_low, recur_low, bias_input, bias_recur, counts, keep
    )
    pooled_low, blocks = land([up_fetch], pooled_low, blocks)
    up_fetch.share()
    down_fetch.cross()
    everyone = jnp.concatenate(blocks, axis=0)
    all_keys, all_values = everyone[:, :width], everyone[:, width:]
    mixed, logsum = attend(queries, all_keys, all_values, seg_q, seg_k, HEAD_DIM)
    (mixed,) = land([up_fetch, down_fetch], mixed)
    up_fetch.swap()
    down_fetch.share()

    output_low, expand_low = up_fetch.whole()
    first_in = widen(token_in) + (dot(mixed, output_low) + bias_output)
    first = layer_norm(first_in, gain_first, shift_first)
    first_low = first.astype(BF16)
    up = dot(first_low, expand_low) + bias_expand
    hidden = gelu_exact(up).astype(BF16)
    (hidden,) = land([down_fetch], hidden)
    down_fetch.swap()
    shrink_low, project_token, project_char = down_fetch.whole()
    token_mid = first + dot(hidden, shrink_low) + bias_shrink
    mid_low = token_mid.astype(BF16)

    tok_side = dot(mid_low, project_token) + bias_token
    char_side = dot(pooled_low, project_char) + bias_char
    joined = jnp.concatenate([tok_side, char_side], axis=1).astype(BF16)
    joined_ext = with_halo(joined)
    merged = (
        bias_merging
        + dot(joined_ext[0:rows], kernel_low[0])
        + dot(joined_ext[1 : rows + 1], kernel_low[1])
        + dot(joined_ext[2 : rows + 2], kernel_low[2])
    )
    act = gelu_exact(merged)
    tok_pre = token_mid + act[:, :width]
    char_pre = widen(char_in) + act[:, width:]
    token_out = layer_norm(tok_pre, gain_token, shift_token).astype(BF16)
    char_out = layer_norm(char_pre, gain_char, shift_char).astype(BF16)

    _, token_pull = jax.vjp(layer_norm, tok_pre, gain_token, shift_token)
    tok_pre_grad, token_gain_grad, token_shift_grad = token_pull(widen(token_cot))
    _, char_pull = jax.vjp(layer_norm, char_pre, gain_char, shift_char)
    char_grad, char_gain_grad, char_shift_grad = char_pull(widen(char_cot))
    act_grad = jnp.concatenate([tok_pre_grad, char_grad], axis=1)
    merged_grad = (act_grad * gelu_slope(merged)).astype(BF16)
    merging_bias_grad = jnp.sum(widen(merged_grad), axis=0)
    exchange = flip(
        jnp.concatenate(
            [joined_ext, jnp.pad(core_half(merged_grad, 1 - core), ((0, 2), (0, 0)))], axis=1
        ),
        1,
    )
    merged_ext = with_halo(merged_grad)
    centre = back_product(merged_grad, kernel_low[1])
    exchange, merged_ext, centre = lax.optimization_barrier((exchange, merged_ext, centre))
    joined_pair = (joined_ext, exchange[:, : 2 * width])
    merged_pair = (core_half(merged_grad, core), exchange[:rows, 2 * width :])
    others = [(place + hop) % parts for hop in range(1, parts)]

    def merging_terms(target):
        sources = columns(joined_pair, target, parts)
        return jnp.concatenate(
            [
                pair_product([item[tap : tap + rows] for item in sources], merged_pair)
                for tap in range(3)
            ],
            axis=0,
        )

    token = jnp.zeros((8, 128), F32)
    merging_flow = Flow([merging_terms(j).astype(BF16) for j in others], merging_terms(place))
    token, (centre, merged_ext) = turn(token, [], [merging_flow], centre, merged_ext)
    joined_grad = (
        back_product(merged_ext[2 : rows + 2], kernel_low[0])
        + centre
        + back_product(merged_ext[0:rows], kernel_low[2])
    )
    tok_side_grad = joined_grad[:, :width].astype(BF16)
    char_side_grad = joined_grad[:, width:].astype(BF16)
    token_bias_grad = jnp.sum(widen(tok_side_grad), axis=0)
    char_bias_grad = jnp.sum(widen(char_side_grad), axis=0)
    pooled_grad = back_product(char_side_grad, project_char)
    mid_grad = tok_pre_grad + back_product(tok_side_grad, project_token)

    shrink_out_grad = mid_grad.astype(BF16)
    shrink_bias_grad = jnp.sum(widen(shrink_out_grad), axis=0)
    hidden_grad = back_product(shrink_out_grad, shrink_low)
    up_grad = (hidden_grad * gelu_slope(up)).astype(BF16)
    expand_bias_grad = jnp.sum(widen(up_grad), axis=0)
    middle_own = jnp.concatenate(
        [
            hidden, first_low, mid_low, pooled_low, shrink_out_grad, up_grad, tok_side_grad,
            char_side_grad,
        ],
        axis=1,
    )
    middle_pair = (middle_own, flip(middle_own, 1))
    first_grad = mid_grad + back_product(up_grad, expand_low)
    _, first_pull = jax.vjp(layer_norm, first_in, gain_first, shift_first)
    first_in_grad, first_gain_grad, first_shift_grad = first_pull(first_grad)
    attn_grad = first_in_grad.astype(BF16)
    output_bias_grad = jnp.sum(widen(attn_grad), axis=0)
    mixed_grad = back_product(attn_grad, output_low).astype(BF16)
    mixed_grad, middle_pair = lax.optimization_barrier((mixed_grad, middle_pair))

    def middle_terms(target, dtype):
        if width // parts == PACK:
            deep = ff // 2 // PACK
            at_first = 2 * deep
            at_mid, at_pooled, at_out, at_up = [at_first + 2 * k for k in range(1, 5)]
            at_tok, at_char = at_up + 2 * deep, at_up + 2 * deep + 2
            left = [target * deep + k for k in range(deep)]
            left += [at_up + core * deep + k for k in range(deep)]
            left += [at_mid + target, at_pooled + target]
            right = [at_out + core] * deep + [at_first + target] * deep
            right += [at_tok + core, at_char + core]
            table = jnp.stack([jnp.stack(left), jnp.stack(right)])
            return block_terms(middle_pair, middle_pair, table, PACK, dtype)
        ends = [ff + width * k for k in range(5)] + [2 * ff + width * k for k in range(4, 7)]
        hiddens, firsts, mids, pools, outs, ups, toks, sides = [
            [item[:, lo:hi] for item in middle_pair] for lo, hi in zip([0] + ends[:-1], ends)
        ]
        outs, ups, toks, sides = [
            [core_half(item, core) for item in pair] for pair in (outs, ups, toks, sides)
        ]
        return pack_rows(
            [
                pair_product(columns(hiddens, target, parts), outs),
                pair_product(ups, columns(firsts, target, parts)),
                pair_product(columns(mids, target, parts), toks),
                pair_product(columns(pools, target, parts), sides),
            ],
            PACK,
            dtype,
        )

    middle_flow = Flow([middle_terms(j, BF16) for j in others], None)
    final = jnp.stack([pooled_grad[:, :hid], pooled_grad[:, hid:]])
    token, (mixed_grad, final) = turn(token, [], [middle_flow], mixed_grad, final)

    queries_grad, *terms = attend_back(
        queries, all_keys, all_values, seg_q, seg_k, mixed_grad, logsum, HEAD_DIM
    )
    token, (final, queries_grad, terms, middle_flow.value) = turn(
        token, [merging_flow], [], final, queries_grad, terms, middle_terms(place, BF16)
    )
    away_terms = [shift_shard(terms[hop], -hop % parts) for hop in range(1, parts)]
    late_own = jnp.concatenate([token_in, mixed, queries_grad, attn_grad], axis=1)
    late_other = flip(late_own, 1)

    own_counts = jnp.stack([counts[2], counts[2]])
    own_grads = gru_backward(
        True, letters[2], letters[2], input_low, recur_low, bias_input, bias_recur, own_counts,
        keep, starts, final,
    )
    token, (own_grads, away_terms, late_other) = turn(
        token, [merging_flow], [], own_grads, away_terms, late_other
    )
    owned = widen(terms[0])
    for item in away_terms:
        owned = owned + widen(item)
    owned = owned.astype(BF16)
    keys_grad, values_grad = owned[0], owned[1]
    owned_other = flip(owned, 1)
    late_pair = (late_own, late_other)

    def late_terms(targets):
        if width // parts == PACK:
            left = jnp.stack([item for j in targets for item in (j, 2 + j)])
            right = jnp.stack([4 + core, 6 + core] * len(targets))
            first = block_terms(late_pair, late_pair, jnp.stack([left, right]), PACK, BF16)
            first, owned_other_now = lax.optimization_barrier((first, owned_other))
            owned_pair = (owned, owned_other_now)
            left = jnp.stack([item for j in targets for item in (j, j)])
            right = jnp.stack([core, 2 + core] * len(targets))
            second = block_terms(late_pair, owned_pair, jnp.stack([left, right]), PACK, BF16)
            deep = 2 * PACK
            return [
                jnp.concatenate([item[k * deep : (k + 1) * deep] for item in (first, second)], axis=0)
                for k in range(len(targets))
            ]
        inputs, mixes, query_part, attn_part = [
            [item[:, k * width : (k + 1) * width] for item in late_pair] for k in range(4)
        ]
        key_part, value_part = [
            [item[k] for item in (owned, owned_other)] for k in range(2)
        ]
        products = (
            (inputs, query_part), (mixes, attn_part), (inputs, key_part), (inputs, value_part)
        )
        return [
            pack_rows(
                [
                    pair_product(columns(one, j, parts), [core_half(item, core) for item in two])
                    for one, two in products
                ],
                PACK,
                BF16,
            )
            for j in targets
        ]

    *late_sent, late_own_terms = late_terms(others + [place])
    late_flow = Flow(late_sent, late_own_terms)
    token, (own_grads,) = turn(token, [], [late_flow], own_grads)

    near_grads = gru_backward(
        False, letters[0], letters[1], input_low, recur_low, bias_input, bias_recur, counts[:2],
        keep, starts, own_grads[2], own_grads[3:],
    )
    token, (own_grads, near_grads) = turn(
        token, [late_flow, merging_flow, middle_flow], [], own_grads, near_grads
    )

    table_grad = table_terms_of(id_columns, *near_grads[:2], *own_grads[:2], vocab)
    query_bias_grad = jnp.sum(widen(queries_grad), axis=0)
    value_bias_grad = jnp.sum(widen(values_grad), axis=0)
    bias_input_grad, bias_recur_grad = near_grads[5:]
    vector_grads = (
        query_bias_grad, value_bias_grad, output_bias_grad, first_gain_grad, first_shift_grad,
        expand_bias_grad, shrink_bias_grad, bias_input_grad[:, 0], bias_recur_grad[:, 0],
        token_bias_grad, char_bias_grad, merging_bias_grad, token_gain_grad, token_shift_grad,
        char_gain_grad, char_shift_grad,
    )
    vector_terms = jnp.concatenate(
        [
            jnp.moveaxis(item.reshape(item.shape[:-1] + (parts, -1)), -2, 0).reshape(parts, -1)
            for item in vector_grads
        ],
        axis=1,
    ).reshape(parts, 2, -1, PACK)
    chars_part, hid_part = chars // parts, hid // parts
    part, joint = width // parts, 2 * width // parts
    tail_rows = vocab // parts // 2
    gru_shapes = [
        (chars_part, gate_width), (hid_part, gate_width), (tail_rows, PACK),
        (vector_terms.shape[2], PACK),
    ]
    depth = sum(deep * lanes for deep, lanes in gru_shapes) // PACK
    depth += -depth % (4 * rep_size())
    table_terms = table_grad.reshape(parts, 2, tail_rows, chars)
    gru_sums = near_grads[3:5]
    gru_away = pack_gru_terms(
        1 - core, gru_sums, table_terms, vector_terms, depth, PACK, BF16
    )
    token, (gru_sums, table_terms, vector_terms, gru_away) = turn(
        token, [late_flow], [], gru_sums, table_terms, vector_terms, gru_away
    )
    gru_away = flip(gru_away, 1)
    gru_own = pack_gru_terms(core, gru_sums, table_terms, vector_terms, depth, PACK, F32)
    token, (gru_own, gru_away) = turn(token, [], [], gru_own, gru_away)
    gru_total = gru_own + widen(gru_away)
    gru_flow = Flow(
        [lax.dynamic_index_in_dim(gru_total, j, 0, keepdims=False).astype(BF16) for j in others],
        lax.dynamic_index_in_dim(gru_total, place, 0, keepdims=False),
    )
    token, (queries_grad, keys_grad, values_grad) = turn(
        token, [], [gru_flow], queries_grad, keys_grad, values_grad
    )
    token_grad = (
        first_in_grad
        + back_product(queries_grad, query_low)
        + back_product(keys_grad, key_low)
        + back_product(values_grad, value_low)
    )
    flows = dict(a=merging_flow, b=middle_flow, c=late_flow, d=gru_flow)
    shapes = dict(
        a=[(3 * joint, width, "lanes")],
        b=[
            (ff // parts, PACK, "lanes"), (ff // 2, part, "turned"), (part, PACK, "lanes"),
            (part, PACK, "lanes"),
        ],
        c=[(part, PACK, "lanes")] * 4,
        d=[
            (chars_part, gate_width, "stacked"), (hid_part, gate_width, "stacked"),
            (tail_rows, chars, "rows"), (vector_terms.shape[2], PACK, "stacked"),
        ],
    )
    owned_shards = {}
    for name in TAIL + "abcd" * 16:
        if name == "d" and len(gru_flow.stages) == 1 and not merging_flow.stages:
            shards_now = weights_of(merging_flow.value, shapes["a"])
            gru_flow.got, owned_shards["a"] = lax.optimization_barrier((gru_flow.got, shards_now))
        token, _ = turn(token, [flows[name]], [])
    for name, flow in flows.items():
        if name not in owned_shards:
            owned_shards[name] = weights_of(flow.value, shapes[name])
    (merging_out,) = owned_shards["a"]
    merging_out = merging_out.reshape(3, joint, 2 * width)
    shrink_out, expand_out, token_proj_out, char_proj_out = owned_shards["b"]
    query_out, output_out, key_out, value_out = owned_shards["c"]
    input_out, recur_out, table_out, flat_out = owned_shards["d"]
    flat_out = flat_out.reshape(-1)
    vector_out, at = [], 0
    for item in vectors:
        vector_out.append(flat_out[at : at + item.size].reshape(item.shape))
        at += item.size
    (
        query_bias_out, value_bias_out, output_bias_out, first_gain_out, first_shift_out,
        expand_bias_out, shrink_bias_out, input_bias_out, recur_bias_out, token_bias_out,
        char_bias_out, merging_bias_out, token_gain_out, token_shift_out, char_gain_out,
        char_shift_out,
    ) = vector_out
    return (
        token_out, char_out, token_grad, char_grad,
        query_out, key_out, value_out, output_out,
        query_bias_out, value_bias_out, output_bias_out, first_gain_out, first_shift_out,
        expand_out, expand_bias_out, shrink_out, shrink_bias_out, table_out,
        input_out, input_bias_out, recur_out, recur_bias_out,
        token_proj_out, token_bias_out, char_proj_out, char_bias_out,
        merging_out, merging_bias_out, token_gain_out, token_shift_out, char_gain_out,
        char_shift_out,
    )


def solution(mesh):
    sizes = (mesh.shape["rep"] // 2, 2, mesh.shape["shard"])
    mesh = jax.sharding.Mesh(mesh.devices.reshape(sizes), ("pair", "core", "shard"))
    rows = P(("pair", "core", "shard"), None)
    split, vector = P("shard", None), P("shard")
    in_specs = (
        rows, rows, rows, P(("pair", "core", "shard")), P(("pair", "core")), rows, rows,
        split, split, split, split, vector, vector, vector, vector, vector,
        split, vector, split, vector, split,
        P(None, "shard", None), P(None, "shard"), P(None, "shard", None), P(None, "shard"),
        split, vector, split, vector, P(None, "shard", None), vector,
        vector, vector, vector, vector,
    )
    out_specs = (rows,) * 4 + in_specs[7:]
    return jax.shard_map(shards, mesh=mesh, in_specs=in_specs, out_specs=out_specs, check_vma=False)
```
